256 devices in a mesh: tiles: 64 (over y, z, core), rep: 4 (over x).
Axes of the slice: x: 4, y: 4, z: 8, core: 2. Of those that a mesh axis runs over, the one named last changes fastest.
Arguments:
- fields: bfloat16 [4, 64, 200, 768], P('rep', 'tiles'), may hold values from -6 to 6
- wet_bits: int32 [64, 6, 5], P('tiles'), may hold values from 0 to 1073741823, as said below
- neighbours: int32 [64, 8], P('tiles'), may hold values from -1 to 63, as said below
- kernel: float32 [200, 49], replicated, may hold values from -0.875 to 0.875
- conv_bias: float32 [200], replicated, may hold values from -3 to 3
- ln_gain: float32 [200], replicated, may hold values from 0.5 to 1.5
- ln_shift: float32 [200], replicated, may hold values from -3 to 3
- in_weight: bfloat16 [200, 800], replicated, may hold values from -0.4375 to 0.4375
- in_bias: float32 [800], replicated, may hold values from -3 to 3
- out_weight: bfloat16 [800, 200], replicated, may hold values from -0.21875 to 0.21875
- out_bias: float32 [200], replicated, may hold values from -3 to 3
- cotangent: bfloat16 [4, 64, 200, 768], P('rep', 'tiles'), may hold values from -6 to 6
Outputs:
- out_field: bfloat16 [4, 64, 200, 768], P('rep', 'tiles')
- input_grad: bfloat16 [4, 64, 200, 768], P('rep', 'tiles')
- grad_kernel: float32 [200, 49], replicated
- grad_conv_bias: float32 [200], replicated
- grad_gain: float32 [200], replicated
- grad_shift: float32 [200], replicated
- grad_in_weight: float32 [200, 800], replicated
- grad_in_bias: float32 [800], replicated
- grad_out_weight: float32 [800, 200], replicated
- grad_out_bias: float32 [200], replicated
The draws below stay inside these ranges and needn't reach their ends.
Inputs may be any that keep to these rules, and one draw needn't show every extreme that they name: `neighbours`: tile slot s lies in band s; the slots of a band sit at increasing columns of a periodic row of 2 tile columns, the other columns being land. Entry k of row s names the slot of the wet tile beside tile s to the north (band - 1), south (band + 1), west, east, north-west, north-east, south-west or south-east (columns taken modulo 2), or -1 where that tile is land or lies beyond the first or last band. `wet_bits`: bit j (j < 30) of word w of row r of tile s is 1 where the cell in column 30 * w + j of that row is wet; bits for columns at or beyond 128 are ignored.
All inputs are finite; a program needn't handle non-finite values.
Results may differ from the reference program's by a relative error of at most 0.006.
Values may be sent and summed in bfloat16 or wider, within the bound.
No kernel may reach another device: no remote copies, remote signals or barrier semaphores. Data moves between devices by JAX's collectives and lax.ppermute only.
A program may use at most 128 MiB of HBM per device.

```python
import jax
import jax.numpy as jnp
from jax import lax

C = 200
HID = 800
KERNEL_DILATION = 2
HALO = 6
TILE_ROWS = 6
TILE_COLUMNS = 128
TPD = 1
GC = 2
NT = 64
CELLS = 768
WORDS = 5
SAMPLES = 4


def tile_geometry(key):
    bands = NT // TPD
    orders = jax.vmap(lambda band_key: jax.random.permutation(band_key, GC))(jax.random.split(key, bands))
    columns = jnp.sort(orders[:, :TPD], axis=1).astype(jnp.int32)
    band_ids = jnp.repeat(jnp.arange(bands, dtype=jnp.int32), TPD)
    slot_ids = jnp.arange(NT, dtype=jnp.int32)
    flat_cols = columns.reshape(NT)
    occupied = jnp.full((bands, GC), -1, jnp.int32).at[band_ids, flat_cols].set(slot_ids)
    band_steps = (-1, 1, 0, 0, -1, -1, 1, 1)
    col_steps = (0, 0, -1, 1, -1, 1, -1, 1)
    result = []
    for k in range(8):
        target_band = band_ids + band_steps[k]
        target_col = (flat_cols + col_steps[k]) % GC
        inside = (target_band >= 0) & (target_band < bands)
        found = occupied[jnp.clip(target_band, 0, bands - 1), target_col]
        result.append(jnp.where(inside, found, -1))
    return jnp.stack(result, axis=1).astype(jnp.int32)


def draw_neighbours(key, part):
    return tile_geometry(jax.random.fold_in(key, 7))


def draw_wet_bits(key, part):
    first_key = jax.random.fold_in(key, 11)
    second_key = jax.random.fold_in(key, 13)
    first_bits = jax.random.randint(first_key, (NT, TILE_ROWS, WORDS), 0, 2 ** 30, dtype=jnp.int32)
    second_bits = jax.random.randint(second_key, (NT, TILE_ROWS, WORDS), 0, 2 ** 30, dtype=jnp.int32)
    return jnp.bitwise_or(first_bits, second_bits)


def steps_of(own_key, shape, cuts, smallest, high):
    level, own = 1.0, jax.random.fold_in(own_key, 6)
    for dim, parts in cuts:
        draws = jnp.exp(jax.random.uniform(jax.random.fold_in(own, dim), (parts,), jnp.float32, smallest / len(cuts), high / len(cuts)))
        level = level * jnp.repeat(draws, shape[dim] // parts).reshape([-1 if axis == dim else 1 for axis in range(len(shape))])
    return level


def gaussian(stream_key, dims, width, limit, cuts=(), kind=jnp.bfloat16):
    drawn = jax.random.normal(stream_key, dims, jnp.float32) * width
    if len(cuts) > 0:
        drawn = steps_of(stream_key, dims, cuts, -0.22, 0.18) * drawn
    return jnp.clip(drawn, min=-limit, max=limit).astype(kind)


def setup_inputs(seed: int = 0) -> dict:
    keys = jax.random.split(jax.random.key(seed), 13)
    fields = gaussian(keys[0], (SAMPLES, NT, C, CELLS), 1.0, 6.0, ((0, 4), (1, 64)))
    wet_bits = draw_wet_bits(jax.random.fold_in(keys[12], 71), 0)
    neighbours = draw_neighbours(jax.random.fold_in(keys[12], 71), 0)
    kernel = gaussian(keys[3], (C, 49), 49 ** -0.5, 0.875, (), jnp.float32)
    conv_bias = gaussian(keys[4], (C,), 0.5, 3.0, (), jnp.float32)
    ln_gain = jnp.clip(jax.random.uniform(keys[5], (C,), jnp.float32, 0.5, 1.5), 0.5, 1.5)
    ln_shift = gaussian(keys[6], (C,), 0.5, 3.0, (), jnp.float32)
    in_weight = gaussian(keys[7], (C, HID), C ** -0.5, 0.4375)
    in_bias = gaussian(keys[8], (HID,), 0.5, 3.0, (), jnp.float32)
    out_weight = gaussian(keys[9], (HID, C), HID ** -0.5, 0.21875)
    out_bias = gaussian(keys[10], (C,), 0.5, 3.0, (), jnp.float32)
    cotangent = gaussian(keys[11], (SAMPLES, NT, C, CELLS), 1.0, 6.0, ((0, 4), (1, 64)))
    return dict(fields=fields, wet_bits=wet_bits, neighbours=neighbours, kernel=kernel, conv_bias=conv_bias, ln_gain=ln_gain, ln_shift=ln_shift, in_weight=in_weight, in_bias=in_bias, out_weight=out_weight, out_bias=out_bias, cotangent=cotangent)


gelu_scale = 0.7978845608028654

def gelu_pair(hidden):
    tanh_arg = gelu_scale * (hidden + 0.044715 * hidden * hidden * hidden)
    tanh_val = jnp.tanh(tanh_arg)
    active = 0.5 * hidden * (1.0 + tanh_val)
    derivative = 0.5 * (1.0 + tanh_val) + 0.5 * hidden * (1.0 - tanh_val * tanh_val) * gelu_scale * (1.0 + 3.0 * 0.044715 * hidden * hidden)
    return (active, derivative)

def unpack_wet(packed, columns):
    spread = jnp.repeat(packed, 30, axis=-1)[..., :columns]
    offsets = jnp.arange(columns, dtype=jnp.int32) % 30
    return jnp.bitwise_and(jnp.right_shift(spread, offsets), 1)

def taps_sum(padded_field, kernel, tile_row_count, tile_column_count):
    summed = jnp.zeros(padded_field.shape[:2] + (tile_row_count, tile_column_count), jnp.float32)
    for first_operand in range(7):
        for second_operand in range(7):
            kernel_window = padded_field[:, :, KERNEL_DILATION * first_operand:KERNEL_DILATION * first_operand + tile_row_count, KERNEL_DILATION * second_operand:KERNEL_DILATION * second_operand + tile_column_count].astype(jnp.float32)
            summed = summed + kernel_window * kernel[:, 7 * first_operand + second_operand][None, :, None, None]
    return summed

def gather_tiles(tile_field, index_list):
    clipped = jnp.clip(index_list, 0, tile_field.shape[0] - 1)
    return jnp.where((index_list >= 0)[:, None, None, None], tile_field[clipped], jnp.zeros((), tile_field.dtype))

def pad_tiles(tile_field, neighbours):
    margin = HALO
    upper_band = jnp.concatenate([gather_tiles(tile_field[:, :, TILE_ROWS - margin:, TILE_COLUMNS - margin:], neighbours[:, 4]), gather_tiles(tile_field[:, :, TILE_ROWS - margin:, :], neighbours[:, 0]), gather_tiles(tile_field[:, :, TILE_ROWS - margin:, :margin], neighbours[:, 5])], axis=3)
    middle = jnp.concatenate([gather_tiles(tile_field[:, :, :, TILE_COLUMNS - margin:], neighbours[:, 2]), tile_field, gather_tiles(tile_field[:, :, :, :margin], neighbours[:, 3])], axis=3)
    lower_band = jnp.concatenate([gather_tiles(tile_field[:, :, :margin, TILE_COLUMNS - margin:], neighbours[:, 6]), gather_tiles(tile_field[:, :, :margin, :], neighbours[:, 1]), gather_tiles(tile_field[:, :, :margin, :margin], neighbours[:, 7])], axis=3)
    return jnp.concatenate([upper_band, middle, lower_band], axis=2)

def reference(fields, wet_bits, neighbours, kernel, conv_bias, ln_gain, ln_shift, in_weight, in_bias, out_weight, out_bias, cotangent):
    wet_mask = unpack_wet(wet_bits, TILE_COLUMNS).astype(jnp.bfloat16)[:, None]
    wet_float = wet_mask.astype(jnp.float32)
    wet_flat = wet_float.reshape(NT, 1, CELLS)

    def one_sample(totals, sample_pair):
        sample_in, sample_cot = sample_pair
        masked = sample_in.reshape(NT, C, TILE_ROWS, TILE_COLUMNS) * wet_mask
        padded_field = pad_tiles(masked, neighbours)
        convolved = conv_bias[None, :, None, None] + taps_sum(padded_field, kernel, TILE_ROWS, TILE_COLUMNS)
        centre_mean = lax.optimization_barrier(jnp.mean(convolved, axis=1, keepdims=True))
        centred = convolved - centre_mean
        inv_std = lax.rsqrt(lax.optimization_barrier(jnp.mean(centred * centred, axis=1, keepdims=True)) + 1e-06)
        normed = centred * inv_std
        normout = (normed * ln_gain[None, :, None, None] + ln_shift[None, :, None, None]).astype(jnp.bfloat16)
        out_grad = sample_cot.reshape(NT, C, TILE_ROWS, TILE_COLUMNS) * wet_mask

        def per_tile(inner, tile_item):
            norm_tile, grad_tile, masked_tile, wet_tile = tile_item
            hidden = jnp.dot(in_weight.T, norm_tile, preferred_element_type=jnp.float32) + in_bias[:, None]
            active, derivative = gelu_pair(hidden)
            active_b = active.astype(jnp.bfloat16)
            update = jnp.dot(out_weight.T, active_b, preferred_element_type=jnp.float32) + out_bias[:, None]
            out_tile = (wet_tile * (masked_tile.astype(jnp.float32) + update)).astype(jnp.bfloat16)
            act_grad = jnp.dot(out_weight, grad_tile, preferred_element_type=jnp.float32)
            hid_grad = (act_grad * derivative).astype(jnp.bfloat16)
            norm_grad = jnp.dot(in_weight, hid_grad, preferred_element_type=jnp.float32)
            inner = (inner[0] + jnp.dot(norm_tile, hid_grad.T, preferred_element_type=jnp.float32), inner[1] + lax.optimization_barrier(jnp.sum(hid_grad.astype(jnp.float32), axis=1)), inner[2] + jnp.dot(active_b, grad_tile.T, preferred_element_type=jnp.float32), inner[3] + lax.optimization_barrier(jnp.sum(grad_tile.astype(jnp.float32), axis=1)))
            return (inner, (out_tile, norm_grad))
        start = (jnp.zeros((C, HID), jnp.float32), jnp.zeros((HID,), jnp.float32), jnp.zeros((HID, C), jnp.float32), jnp.zeros((C,), jnp.float32))
        mixer, (out_tiles, norm_grad) = lax.scan(per_tile, start, (normout.reshape(NT, C, CELLS), out_grad.reshape(NT, C, CELLS), masked.reshape(NT, C, CELLS), wet_flat))
        norm_grad = norm_grad.reshape(NT, C, TILE_ROWS, TILE_COLUMNS)
        scaled_grad = norm_grad * ln_gain[None, :, None, None]
        conv_grad = (inv_std * (scaled_grad - lax.optimization_barrier(jnp.mean(scaled_grad, axis=1, keepdims=True)) - normed * lax.optimization_barrier(jnp.mean(scaled_grad * normed, axis=1, keepdims=True)))).astype(jnp.bfloat16)
        conv_float = conv_grad.astype(jnp.float32)
        kernel_cols = []
        for first_operand in range(7):
            for second_operand in range(7):
                kernel_window = padded_field[:, :, KERNEL_DILATION * first_operand:KERNEL_DILATION * first_operand + TILE_ROWS, KERNEL_DILATION * second_operand:KERNEL_DILATION * second_operand + TILE_COLUMNS].astype(jnp.float32)
                kernel_cols.append(lax.optimization_barrier(jnp.sum(conv_float * kernel_window, axis=(0, 2, 3))))
        kernel_grad = jnp.stack(kernel_cols, axis=1)

        def conv_of(grid_in):
            return taps_sum(pad_tiles(grid_in, neighbours), kernel, TILE_ROWS, TILE_COLUMNS)
        _, pullback = jax.vjp(conv_of, masked.astype(jnp.float32))
        mask_grad, = pullback(conv_float)
        input_grad = (wet_float * (out_grad.astype(jnp.float32) + mask_grad)).astype(jnp.bfloat16)
        totals = (totals[0] + kernel_grad, totals[1] + lax.optimization_barrier(jnp.sum(conv_float, axis=(0, 2, 3))), totals[2] + lax.optimization_barrier(jnp.sum(norm_grad * normed, axis=(0, 2, 3))), totals[3] + lax.optimization_barrier(jnp.sum(norm_grad, axis=(0, 2, 3))), totals[4] + mixer[0], totals[5] + mixer[1], totals[6] + mixer[2], totals[7] + mixer[3])
        return (totals, (out_tiles, input_grad.reshape(NT, C, CELLS)))
    init = (jnp.zeros((C, 49), jnp.float32), jnp.zeros((C,), jnp.float32), jnp.zeros((C,), jnp.float32), jnp.zeros((C,), jnp.float32), jnp.zeros((C, HID), jnp.float32), jnp.zeros((HID,), jnp.float32), jnp.zeros((HID, C), jnp.float32), jnp.zeros((C,), jnp.float32))
    totals, (out_field, input_grad) = lax.scan(one_sample, init, (fields, cotangent))
    norm_factor = (SAMPLES * NT * CELLS) ** (-0.5)
    return (out_field, input_grad, totals[0] * norm_factor, totals[1] * norm_factor, totals[2] * norm_factor, totals[3] * norm_factor, totals[4] * norm_factor, totals[5] * norm_factor, totals[6] * norm_factor, totals[7] * norm_factor)
```

```python
import jax
import jax.numpy as jnp
from jax import lax
from jax.experimental import pallas as pl
from jax.experimental.pallas import tpu as pltpu
from jax.sharding import Mesh, PartitionSpec as P

C = 200
CX = 208
HID = 800
ROWS = 6
COLS = 128
CELLS = 768
WORDS = 5
BITS = 30
GROUPS = C // 8
IN_BLOCKS = 7
OUT_BASE = IN_BLOCKS * CX
PACK = 3072
SMALL = C - 128
BIAS_LANES = 49

bf16 = jnp.bfloat16
f32 = jnp.float32
gelu_scale = 0.7978845608028654
VMEM = pl.BlockSpec(memory_space=pltpu.VMEM)
SMEM = pl.BlockSpec(memory_space=pltpu.SMEM)
NT_DIMS = (((1,), (1,)), ((), ()))


def row_class(row):
    return row // ROWS


def lanes(r):
    return slice(r * COLS, (r + 1) * COLS)


def wet_row(bits_ref, r):
    col = lax.broadcasted_iota(jnp.int32, (8, COLS), 1)
    word = jnp.zeros((8, COLS), jnp.int32)
    shift = col
    for w in range(WORDS):
        word = jnp.where(col >= BITS * w, bits_ref[r, w], word)
        shift = jnp.where(col >= BITS * w, col - BITS * w, shift)
    return jnp.bitwise_and(jnp.right_shift(word, shift), 1).astype(f32)


def mask_kernel(bits_ref, fields_ref, masked_ref, wet_ref):
    for r in range(ROWS):
        wet = wet_row(bits_ref, r)
        wet_ref[:, lanes(r)] = wet
        masked_ref[:, lanes(r)] = (fields_ref[:, lanes(r)].astype(f32) * wet[0:1]).astype(bf16)


def fill_masks(slot_ref, near_ref, masks_ref):
    slot = slot_ref[0]

    def flag(k, step):
        return jnp.where(near_ref[0, k] == slot + step, 1.0, 0.0).astype(f32)

    lane = lax.broadcasted_iota(jnp.int32, (8, COLS), 1)
    triples = (
        (flag(0, -1), flag(4, -1), flag(5, -1)),
        (jnp.float32(1.0), flag(2, 0), flag(3, 0)),
        (flag(1, 1), flag(6, 1), flag(7, 1)),
    )
    for cls, (centre, west, east) in enumerate(triples):
        for b in range(7):
            off = 2 * b - 6
            mask = jnp.full((8, COLS), centre, f32)
            if off > 0:
                mask = jnp.where(lane < off, jnp.full((8, COLS), east, f32), mask)
            if off < 0:
                mask = jnp.where(lane >= COLS + off, jnp.full((8, COLS), west, f32), mask)
            masks_ref[7 * cls + b] = mask


def fill_rows(north_ref, own_ref, south_ref, rows_ref):
    for part, ref in enumerate((north_ref, own_ref, south_ref)):
        for r in range(ROWS):
            rows_ref[ROWS * part + r] = ref[:, lanes(r)].astype(f32)


def conv_group(rows, taps, masks_ref, flip):
    total = [None] * ROWS
    for b in range(7):
        off = 2 * b - 6
        masked = [rows[r] * masks_ref[7 * row_class(r) + b] for r in range(3 * ROWS)]
        coef = []
        for a in range(7):
            t = 7 * (6 - a) + (6 - b) if flip else 7 * a + b
            coef.append(jnp.broadcast_to(taps[:, t : t + 1], (8, COLS)))
        for i in range(ROWS):
            acc = coef[0] * masked[i]
            for a in range(1, 7):
                acc = acc + coef[a] * masked[i + 2 * a]
            if off != 0:
                acc = pltpu.roll(acc, (-off) % COLS, 1)
            total[i] = acc if total[i] is None else total[i] + acc
    return total


def main_kernel(
    slot_ref,
    near_ref,
    own_ref,
    north_ref,
    south_ref,
    wet_ref,
    cot_ref,
    kern_ref,
    chan_ref,
    inw_ref,
    inwt_ref,
    outw_ref,
    outwt_ref,
    field_ref,
    cgrad_ref,
    norm_ref,
    act_ref,
    hgrad_ref,
    ograd_ref,
    sums_ref,
    rows_ref,
    masks_ref,
    conv_ref,
    istd_ref,
    hid_ref,
    agrad_ref,
):
    fill_masks(slot_ref, near_ref, masks_ref)
    fill_rows(north_ref, own_ref, south_ref, rows_ref)

    osum = jnp.zeros((C, COLS), f32)
    for r in range(ROWS):
        og = cot_ref[:, lanes(r)].astype(f32) * wet_ref[0:1, lanes(r)]
        osum = osum + og
        ograd_ref[:, lanes(r)] = jnp.concatenate([og, jnp.zeros((256 - C, COLS), f32)], axis=0).astype(bf16)
    sums_ref[3] = osum
    agrad_ref[...] = jnp.dot(outw_ref[...], ograd_ref[0:C, :], preferred_element_type=f32)

    def conv_step(g, carry):
        start = pl.multiple_of(g * 8, 8)
        rows = [rows_ref[r, pl.ds(start, 8), :] for r in range(3 * ROWS)]
        taps = kern_ref[pl.ds(start, 8), :]
        total = conv_group(rows, taps, masks_ref, False)
        bias = jnp.broadcast_to(chan_ref[pl.ds(start, 8), 0:1], (8, COLS))
        for i in range(ROWS):
            conv_ref[pl.ds(start, 8), lanes(i)] = total[i] + bias
        return carry

    lax.fori_loop(0, GROUPS, conv_step, 0)

    gain = chan_ref[:, 1:2]
    shift = chan_ref[:, 2:3]
    obias = chan_ref[:, 3:4]
    extra = lax.broadcasted_iota(jnp.int32, (8, COLS), 0)
    extra = jnp.where(extra < 2, 1.0, 0.0).astype(f32)
    for r in range(ROWS):
        x = conv_ref[:, lanes(r)]
        mean = jnp.sum(x, axis=0, keepdims=True) * (1.0 / C)
        x = x - mean
        var = jnp.sum(x * x, axis=0, keepdims=True) * (1.0 / C)
        istd = lax.rsqrt(var + 1e-06)
        normed = x * istd
        conv_ref[:, lanes(r)] = normed
        istd_ref[:, lanes(r)] = jnp.broadcast_to(istd, (8, COLS))
        no = jnp.concatenate([normed * gain + shift, extra], axis=0)
        norm_ref[:, lanes(r)] = no.astype(bf16)

    hid_ref[...] = jnp.dot(inwt_ref[...], norm_ref[...], preferred_element_type=f32)

    def gelu_step(i, carry):
        at = pl.ds(pl.multiple_of(i * 16, 16), 16)
        h = hid_ref[at, :]
        h2 = h * h
        t = jnp.tanh(h * (gelu_scale + (gelu_scale * 0.044715) * h2))
        half = 0.5 + 0.5 * t
        act_ref[at, :] = (h * half).astype(bf16)
        slope = (0.5 * gelu_scale) + (0.5 * gelu_scale * 3.0 * 0.044715) * h2
        deriv = half + h * (1.0 - t * t) * slope
        hgrad_ref[at, :] = (agrad_ref[at, :] * deriv).astype(bf16)
        return carry

    lax.fori_loop(0, HID // 16, gelu_step, 0)

    hid_ref[0:C, :] = jnp.dot(outwt_ref[...], act_ref[...], preferred_element_type=f32)
    agrad_ref[0:C, :] = jnp.dot(inw_ref[...], hgrad_ref[...], preferred_element_type=f32)

    gsum = jnp.zeros((C, COLS), f32)
    ssum = jnp.zeros((C, COLS), f32)
    bsum = jnp.zeros((C, COLS), f32)
    for r in range(ROWS):
        wet = wet_ref[0:1, lanes(r)]
        update = hid_ref[0:C, lanes(r)] + obias
        field_ref[:, lanes(r)] = (wet * (own_ref[:, lanes(r)].astype(f32) + update)).astype(bf16)
        ng = agrad_ref[0:C, lanes(r)]
        normed = conv_ref[:, lanes(r)]
        ssum = ssum + ng
        gsum = gsum + ng * normed
        scaled = ng * gain
        m1 = jnp.sum(scaled, axis=0, keepdims=True) * (1.0 / C)
        m2 = jnp.sum(scaled * normed, axis=0, keepdims=True) * (1.0 / C)
        cg = (istd_ref[0:1, lanes(r)] * (scaled - m1 - normed * m2)).astype(bf16)
        cgrad_ref[:, lanes(r)] = cg
        bsum = bsum + cg.astype(f32)
    sums_ref[0] = bsum
    sums_ref[1] = gsum
    sums_ref[2] = ssum


def grads_kernel(
    slot_ref,
    near_ref,
    own_ref,
    north_ref,
    south_ref,
    cgrad_ref,
    norm_ref,
    act_ref,
    hgrad_ref,
    ograd_ref,
    sums_ref,
    pack_ref,
    rows_ref,
    masks_ref,
    small_ref,
):
    fill_masks(slot_ref, near_ref, masks_ref)
    fill_rows(north_ref, own_ref, south_ref, rows_ref)
    cg_base = 3 * ROWS
    for r in range(ROWS):
        rows_ref[cg_base + r] = cgrad_ref[:, lanes(r)].astype(f32)

    def tap_step(g, carry):
        start = pl.multiple_of(g * 8, 8)
        at = pl.ds(start, 8)
        lane = lax.broadcasted_iota(jnp.int32, (8, COLS), 1)
        small = jnp.zeros((8, COLS), f32)
        for b in range(7):
            off = 2 * b - 6
            acc = [None] * 7
            for i in range(ROWS):
                turned = rows_ref[cg_base + i, at, :]
                if off != 0:
                    turned = pltpu.roll(turned, off % COLS, 1)
                parts = [turned * masks_ref[7 * cls + b] for cls in range(3)]
                for a in range(7):
                    r = i + 2 * a
                    term = parts[row_class(r)] * rows_ref[r, at, :]
                    acc[a] = term if acc[a] is None else acc[a] + term
            for a in range(7):
                value = jnp.sum(acc[a], axis=1, keepdims=True)
                small = jnp.where(lane == SMALL + 7 * a + b, value, small)
        for s in range(4):
            value = jnp.sum(sums_ref[s, at, :], axis=1, keepdims=True)
            small = jnp.where(lane == SMALL + BIAS_LANES + s, value, small)
        small_ref[at, :] = small
        return carry

    lax.fori_loop(0, GROUPS, tap_step, 0)

    for blk in range(IN_BLOCKS):
        first, last = blk * COLS, min((blk + 1) * COLS, HID)
        part = lax.dot_general(norm_ref[...], hgrad_ref[first:last, :], NT_DIMS, preferred_element_type=f32)
        if last - first < COLS:
            part = jnp.concatenate([part, jnp.zeros((CX, COLS - (last - first)), f32)], axis=1)
        pack_ref[blk * CX : (blk + 1) * CX, :] = part.astype(bf16)
    whole = lax.dot_general(act_ref[...], ograd_ref[...], NT_DIMS, preferred_element_type=f32)
    pack_ref[OUT_BASE : OUT_BASE + HID, :] = whole[:, 0:COLS].astype(bf16)
    second = OUT_BASE + HID
    small = jnp.concatenate([small_ref[...], jnp.zeros((8, COLS), f32)], axis=0)
    pack_ref[second : second + CX, :] = (whole[0:CX, COLS:] + small).astype(bf16)
    pack_ref[second + CX : second + HID, :] = whole[CX:, COLS:].astype(bf16)
    pack_ref[second + HID :, :] = jnp.zeros((PACK - second - HID, COLS), bf16)


def back_kernel(
    slot_ref,
    near_ref,
    own_ref,
    north_ref,
    south_ref,
    wet_ref,
    cot_ref,
    kern_ref,
    igrad_ref,
    rows_ref,
    masks_ref,
    conv_ref,
):
    fill_masks(slot_ref, near_ref, masks_ref)
    fill_rows(north_ref, own_ref, south_ref, rows_ref)

    def conv_step(g, carry):
        start = pl.multiple_of(g * 8, 8)
        rows = [rows_ref[r, pl.ds(start, 8), :] for r in range(3 * ROWS)]
        taps = kern_ref[pl.ds(start, 8), :]
        total = conv_group(rows, taps, masks_ref, True)
        for i in range(ROWS):
            conv_ref[pl.ds(start, 8), lanes(i)] = total[i]
        return carry

    lax.fori_loop(0, GROUPS, conv_step, 0)
    for r in range(ROWS):
        wet = wet_ref[0:1, lanes(r)]
        og = cot_ref[:, lanes(r)].astype(f32) * wet
        igrad_ref[:, lanes(r)] = (wet * (og + conv_ref[:, lanes(r)])).astype(bf16)


def unpack_kernel(factor, core_ref, mine_ref, other_ref, gin_ref, gout_ref, gsmall_ref, gvec_ref, full_ref):
    half = PACK // 2
    first = core_ref[0] == 0

    @pl.when(first)
    def _():
        full_ref[0:half, :] = mine_ref[...].astype(f32) * factor
        full_ref[half:, :] = other_ref[...].astype(f32) * factor

    @pl.when(jnp.logical_not(first))
    def _():
        full_ref[0:half, :] = other_ref[...].astype(f32) * factor
        full_ref[half:, :] = mine_ref[...].astype(f32) * factor

    for blk in range(IN_BLOCKS):
        begin, end = blk * COLS, min((blk + 1) * COLS, HID)
        gin_ref[:, begin:end] = full_ref[blk * CX : blk * CX + C, 0 : end - begin]
        gvec_ref[4:5, begin:end] = full_ref[blk * CX + C : blk * CX + C + 1, 0 : end - begin]
    second = OUT_BASE + HID
    gout_ref[:, 0:COLS] = full_ref[OUT_BASE:second, :]
    gout_ref[:, COLS:C] = full_ref[second : second + HID, 0:SMALL]
    gsmall_ref[...] = full_ref[second : second + C, SMALL : SMALL + 49]
    columns = full_ref[second : second + C, :].T
    gvec_ref[0:4, 0:C] = columns[SMALL + BIAS_LANES : SMALL + BIAS_LANES + 4, :]


def call(kernel, outs, n_smem, n_in, scratch=(), flops=0, name=None):
    return pl.pallas_call(
        kernel,
        out_shape=[jax.ShapeDtypeStruct(s, d) for s, d in outs],
        in_specs=[SMEM] * n_smem + [VMEM] * (n_in - n_smem),
        out_specs=[VMEM] * len(outs),
        scratch_shapes=[pltpu.VMEM(s, d) for s, d in scratch],
        cost_estimate=pl.CostEstimate(flops=flops, bytes_accessed=4000000, transcendentals=0),
        name=name,
    )


TILE_AXES = ("y", "z", "core")
PLANE = ("y", "rep")


def shifted(value, steps):
    count = lax.axis_size(TILE_AXES)
    first, last = max(0, -steps), min(count, count - steps)
    return lax.ppermute(value, TILE_AXES, [(s, s + steps) for s in range(first, last)])


def exchange(value, axes):
    return lax.all_to_all(value, axes, 0, 0, tiled=True)


def spread(value, axes):
    count = lax.axis_size(axes)
    rows = value.shape[0]
    return exchange(jnp.broadcast_to(value[None], (count, rows, COLS)).reshape(count * rows, COLS), axes)


def summed(value, count):
    rows = value.shape[0] // count
    return jnp.sum(value.reshape(count, rows, COLS).astype(f32), axis=0).astype(bf16)


def reduce_pack(pack, core):
    half = PACK // 2
    swap = [(0, 1), (1, 0)]
    mine = lax.dynamic_slice_in_dim(pack, core * half, half, 0)
    other = lax.dynamic_slice_in_dim(pack, (1 - core) * half, half, 0)
    got = lax.ppermute(other, "core", swap)
    pair = (mine.astype(f32) + got.astype(f32)).astype(bf16)
    count = lax.axis_size(PLANE)
    part = summed(exchange(pair, PLANE), count)
    part = summed(spread(part, "z"), lax.axis_size("z"))
    mine = spread(part, PLANE)
    return mine, lax.ppermute(mine, "core", swap)


def body(
    fields,
    wet_bits,
    neighbours,
    kernel,
    conv_bias,
    ln_gain,
    ln_shift,
    in_weight,
    in_bias,
    out_weight,
    out_bias,
    cotangent,
):
    act2 = (C, CELLS)
    slot = lax.axis_index(TILE_AXES).astype(jnp.int32).reshape(1)
    core = lax.axis_index("core").astype(jnp.int32)
    cot = cotangent.reshape(act2)
    masked, wet = call(mask_kernel, [(act2, bf16), ((8, CELLS), f32)], 1, 2, name="mask")(
        wet_bits.reshape(ROWS, WORDS), fields.reshape(act2)
    )
    from_north = shifted(masked, 1)
    from_south = shifted(masked, -1)
    chan = jnp.stack([conv_bias, ln_gain, ln_shift, out_bias], axis=1)
    high = lax.reduce_precision(in_bias, 8, 7)
    bias_rows = jnp.stack([high, in_bias - high]).astype(bf16)
    inwt = jnp.concatenate([in_weight, bias_rows, jnp.zeros((CX - C - 2, HID), bf16)], axis=0).T
    field, cgrad, norm, act, hgrad, ograd, sums = call(
        main_kernel,
        [
            (act2, bf16),
            (act2, bf16),
            ((CX, CELLS), bf16),
            ((HID, CELLS), bf16),
            ((HID, CELLS), bf16),
            ((256, CELLS), bf16),
            ((4, C, COLS), f32),
        ],
        2,
        13,
        [
            ((3 * ROWS, C, COLS), f32),
            ((21, 8, COLS), f32),
            (act2, f32),
            ((8, CELLS), f32),
            ((HID, CELLS), f32),
            ((HID, CELLS), f32),
        ],
        flops=10**10,
        name="main",
    )(
        slot,
        neighbours,
        masked,
        from_north,
        from_south,
        wet,
        cot,
        kernel,
        chan,
        in_weight,
        inwt,
        out_weight,
        out_weight.T,
    )
    cg_north = shifted(cgrad, 1)
    cg_south = shifted(cgrad, -1)
    (pack,) = call(
        grads_kernel,
        [((PACK, COLS), bf16)],
        2,
        11,
        [((4 * ROWS, C, COLS), f32), ((21, 8, COLS), f32), ((C, COLS), f32)],
        flops=5 * 10**9,
        name="grads",
    )(slot, neighbours, masked, from_north, from_south, cgrad, norm, act, hgrad, ograd, sums)
    (input_grad,) = call(
        back_kernel,
        [(act2, bf16)],
        2,
        8,
        [((3 * ROWS, C, COLS), f32), ((21, 8, COLS), f32), (act2, f32)],
        flops=3 * 10**9,
        name="back",
    )(slot, neighbours, cgrad, cg_north, cg_south, wet, cot, kernel)
    mine, other = reduce_pack(pack, core)
    total_cells = lax.axis_size(TILE_AXES) * lax.axis_size("rep") * CELLS
    factor = float(total_cells) ** -0.5
    gin, gout, gsmall, gvec = call(
        lambda *refs: unpack_kernel(factor, *refs),
        [((C, HID), f32), ((HID, C), f32), ((C, 49), f32), ((8, HID), f32)],
        1,
        3,
        [((PACK, COLS), f32)],
        flops=10**8,
        name="unpack",
    )(core.reshape(1), mine, other)
    return (
        field.reshape(1, 1, C, CELLS),
        input_grad.reshape(1, 1, C, CELLS),
        gsmall,
        gvec[0, 0:C],
        gvec[1, 0:C],
        gvec[2, 0:C],
        gin,
        gvec[4],
        gout,
        gvec[3, 0:C],
    )


def solution(mesh):
    rep = mesh.shape["rep"]
    fine = Mesh(mesh.devices.reshape(4, -1, 2, rep), ("y", "z", "core", "rep"))
    tile = P("rep", TILE_AXES, None, None)
    placed = (tile, P(TILE_AXES, None, None), P(TILE_AXES, None)) + (P(),) * 8 + (tile,)
    return jax.shard_map(
        body,
        mesh=fine,
        in_specs=placed,
        out_specs=(tile, tile) + (P(),) * 8,
        check_vma=False,
    )
```

```python
import jax
import jax.numpy as jnp
from jax import lax
from jax.experimental import pallas as pl
from jax.experimental.pallas import tpu as pltpu
from jax.sharding import Mesh, PartitionSpec as P


C = 200
CX = 208
HID = 800
ROWS = 6
COLS = 128
CELLS = 768
WORDS = 5
BITS = 30
TAPS = 49
GROUPS = C // 8
BLOCKS = 7
HALF = 1536
SMALL = HID - 6 * COLS
VECTORS = SMALL + TAPS
MIB = 1 << 20

bf16 = jnp.bfloat16
f32 = jnp.float32
gelu_scale = 0.7978845608028654
VMEM = pl.BlockSpec(memory_space=pltpu.VMEM)
SMEM = pl.BlockSpec(memory_space=pltpu.SMEM)
NT_DIMS = (((1,), (1,)), ((), ()))
NORTH, OWN, SOUTH = 0, 1, 2


def row_class(row):
    return row // ROWS


def lanes(r):
    return slice(r * COLS, (r + 1) * COLS)


def wet_row(bits_ref, r):
    col = lax.broadcasted_iota(jnp.int32, (8, COLS), 1)
    word = jnp.zeros((8, COLS), jnp.int32)
    shift = col
    for w in range(WORDS):
        word = jnp.where(col >= BITS * w, bits_ref[w, 0, r], word)
        shift = jnp.where(col >= BITS * w, col - BITS * w, shift)
    return jnp.bitwise_and(jnp.right_shift(word, shift), 1).astype(f32)


def mask_kernel(bits_ref, fields_ref, masked_ref, wet_ref):
    for r in range(ROWS):
        wet = wet_row(bits_ref, r)
        wet_ref[:, lanes(r)] = wet
        masked_ref[:, lanes(r)] = (fields_ref[:, lanes(r)].astype(f32) * wet[0:1]).astype(bf16)


def fill_masks(slot_ref, near_ref, masks_ref):
    slot = slot_ref[0]

    def flag(k, step):
        return jnp.where(near_ref[0, k] == slot + step, 1.0, 0.0).astype(f32)

    lane = lax.broadcasted_iota(jnp.int32, (8, COLS), 1)
    triples = (
        (flag(0, -1), flag(4, -1), flag(5, -1)),
        (jnp.float32(1.0), flag(2, 0), flag(3, 0)),
        (flag(1, 1), flag(6, 1), flag(7, 1)),
    )
    for cls, (centre, west, east) in enumerate(triples):
        for b in range(7):
            off = 2 * b - 6
            mask = jnp.full((8, COLS), centre, f32)
            if off > 0:
                mask = jnp.where(lane < off, jnp.full((8, COLS), east, f32), mask)
            if off < 0:
                mask = jnp.where(lane >= COLS + off, jnp.full((8, COLS), west, f32), mask)
            masks_ref[7 * cls + b] = mask


def fill_rows(ref, part, rows_ref):
    for r in range(ROWS):
        rows_ref[ROWS * part + r] = ref[:, lanes(r)].astype(f32)


def conv_group(rows, coef, masks_ref, classes):
    total = [None] * ROWS
    for b in range(7):
        off = 2 * b - 6
        masked = {}
        for r in rows:
            plain = b == 3 and row_class(r) == OWN
            masked[r] = rows[r] if plain else rows[r] * masks_ref[7 * row_class(r) + b]
        taps = [coef(a, b) for a in range(7)]
        for i in range(ROWS):
            acc = None
            for a in range(7):
                if row_class(i + 2 * a) in classes:
                    term = taps[a] * masked[i + 2 * a]
                    acc = term if acc is None else acc + term
            if off != 0:
                acc = pltpu.roll(acc, (-off) % COLS, 1)
            total[i] = acc if total[i] is None else total[i] + acc
    return total


def pre_kernel(
    slot_ref,
    near_ref,
    own_ref,
    wet_ref,
    cot_ref,
    kern_ref,
    chan_ref,
    outw_ref,
    masks_ref,
    coef_ref,
    chans_ref,
    part_ref,
    ograd_ref,
    agrad_ref,
    osum_ref,
    rows_ref,
):
    fill_masks(slot_ref, near_ref, masks_ref)
    fill_rows(own_ref, 0, rows_ref)
    osum = jnp.zeros((C, COLS), f32)
    for r in range(ROWS):
        og = cot_ref[:, lanes(r)].astype(f32) * wet_ref[0:1, lanes(r)]
        osum = osum + og
        ograd_ref[:, lanes(r)] = jnp.concatenate([og, jnp.zeros((CX - C, COLS), f32)], axis=0).astype(bf16)
    osum_ref[...] = osum
    agrad_ref[...] = jnp.dot(outw_ref[...], ograd_ref[0:C, :], preferred_element_type=f32)

    def step(g, carry):
        at = pl.ds(pl.multiple_of(g * 8, 8), 8)
        kern = kern_ref[at, :]
        chan = chan_ref[at, :]
        for k in range(4):
            chans_ref[k, at, :] = jnp.broadcast_to(chan[:, k : k + 1], (8, COLS))
        rows = {ROWS + r: rows_ref[r, at, :] for r in range(ROWS)}

        def coef(a, b):
            t = 7 * a + b
            tap = jnp.broadcast_to(kern[:, t : t + 1], (8, COLS))
            coef_ref[t, at, :] = tap
            return tap

        total = conv_group(rows, coef, masks_ref, (OWN,))
        for i in range(ROWS):
            part_ref[at, lanes(i)] = total[i] + chans_ref[0, at, :]
        return carry

    lax.fori_loop(0, GROUPS, step, 0)


def main_kernel(
    core_ref,
    own_ref,
    north_ref,
    south_ref,
    wet_ref,
    masks_ref,
    coef_ref,
    chans_ref,
    part_ref,
    ograd_ref,
    agrad_ref,
    osum_ref,
    inw_ref,
    inwt_ref,
    outwt_ref,
    field_ref,
    cgrad_ref,
    keep_ref,
    send_ref,
    rows_ref,
    conv_ref,
    istd_ref,
    hid_ref,
    norm_ref,
    act_ref,
    hgrad_ref,
    sums_ref,
    pack_ref,
):
    fill_rows(north_ref, NORTH, rows_ref)
    fill_rows(own_ref, OWN, rows_ref)
    fill_rows(south_ref, SOUTH, rows_ref)

    def conv_step(g, carry):
        at = pl.ds(pl.multiple_of(g * 8, 8), 8)
        rows = {r: rows_ref[r, at, :] for r in range(3 * ROWS) if row_class(r) != OWN}
        total = conv_group(rows, lambda a, b: coef_ref[7 * a + b, at, :], masks_ref, (NORTH, SOUTH))
        for i in range(ROWS):
            conv_ref[at, lanes(i)] = total[i] + part_ref[at, lanes(i)]
        return carry

    lax.fori_loop(0, GROUPS, conv_step, 0)

    extra = lax.broadcasted_iota(jnp.int32, (8, COLS), 0)
    extra = jnp.where(extra < 2, 1.0, 0.0).astype(f32)
    for r in range(ROWS):
        x = conv_ref[:, lanes(r)]
        mean = jnp.sum(x, axis=0, keepdims=True) * (1.0 / C)
        x = x - mean
        var = jnp.sum(x * x, axis=0, keepdims=True) * (1.0 / C)
        istd = lax.rsqrt(var + 1e-06)
        normed = x * istd
        conv_ref[:, lanes(r)] = normed
        istd_ref[:, lanes(r)] = jnp.broadcast_to(istd, (8, COLS))
        no = jnp.concatenate([normed * chans_ref[1] + chans_ref[2], extra], axis=0)
        norm_ref[:, lanes(r)] = no.astype(bf16)

    hid_ref[...] = jnp.dot(inwt_ref[...], norm_ref[...], preferred_element_type=f32)

    def gelu_step(i, carry):
        at = pl.ds(pl.multiple_of(i * 16, 16), 16)
        h = hid_ref[at, :]
        h2 = h * h
        t = jnp.tanh(h * (gelu_scale + (gelu_scale * 0.044715) * h2))
        half = 0.5 + 0.5 * t
        act_ref[at, :] = (h * half).astype(bf16)
        slope = (0.5 * gelu_scale) + (0.5 * gelu_scale * 3.0 * 0.044715) * h2
        deriv = half + h * (1.0 - t * t) * slope
        hgrad_ref[at, :] = (agrad_ref[at, :] * deriv).astype(bf16)
        return carry

    lax.fori_loop(0, HID // 16, gelu_step, 0, unroll=2)

    hid_ref[0:C, :] = jnp.dot(inw_ref[...], hgrad_ref[...], preferred_element_type=f32)
    gsum = jnp.zeros((C, COLS), f32)
    ssum = jnp.zeros((C, COLS), f32)
    bsum = jnp.zeros((C, COLS), f32)
    cg_base = 3 * ROWS
    for r in range(ROWS):
        ng = hid_ref[0:C, lanes(r)]
        normed = conv_ref[:, lanes(r)]
        ssum = ssum + ng
        gsum = gsum + ng * normed
        scaled = ng * chans_ref[1]
        m1 = jnp.sum(scaled, axis=0, keepdims=True) * (1.0 / C)
        m2 = jnp.sum(scaled * normed, axis=0, keepdims=True) * (1.0 / C)
        cg = (istd_ref[0:1, lanes(r)] * (scaled - m1 - normed * m2)).astype(bf16)
        cgrad_ref[:, lanes(r)] = cg
        rows_ref[cg_base + r] = cg.astype(f32)
        bsum = bsum + cg.astype(f32)
    sums_ref[0] = bsum
    sums_ref[1] = gsum
    sums_ref[2] = ssum
    sums_ref[3] = osum_ref[...]

    hid_ref[0:C, :] = jnp.dot(outwt_ref[...], act_ref[...], preferred_element_type=f32)
    for r in range(ROWS):
        wet = wet_ref[0:1, lanes(r)]
        update = hid_ref[0:C, lanes(r)] + chans_ref[3]
        field_ref[:, lanes(r)] = (wet * (own_ref[:, lanes(r)].astype(f32) + update)).astype(bf16)

    def tap_step(g, carry):
        at = pl.ds(pl.multiple_of(g * 8, 8), 8)
        lane = lax.broadcasted_iota(jnp.int32, (8, COLS), 1)
        small = jnp.zeros((8, COLS), f32)
        for b in range(7):
            off = 2 * b - 6
            acc = [None] * 7
            for i in range(ROWS):
                turned = rows_ref[cg_base + i, at, :]
                if off != 0:
                    turned = pltpu.roll(turned, off % COLS, 1)
                parts = [turned if b == 3 and cls == OWN else turned * masks_ref[7 * cls + b] for cls in range(3)]
                for a in range(7):
                    r = i + 2 * a
                    term = parts[row_class(r)] * rows_ref[r, at, :]
                    acc[a] = term if acc[a] is None else acc[a] + term
            for a in range(7):
                value = jnp.sum(acc[a], axis=1, keepdims=True)
                small = jnp.where(lane == SMALL + 7 * a + b, value, small)
        for s in range(4):
            value = jnp.sum(sums_ref[s, at, :], axis=1, keepdims=True)
            small = jnp.where(lane == VECTORS + s, value, small)
        conv_ref[at, 0:COLS] = small
        return carry

    lax.fori_loop(0, GROUPS, tap_step, 0)

    for half, (left_ref, right_ref) in enumerate(((norm_ref, hgrad_ref), (ograd_ref, act_ref))):
        for blk in range(BLOCKS):
            first, last = blk * COLS, min((blk + 1) * COLS, HID)
            part = lax.dot_general(left_ref[...], right_ref[first:last, :], NT_DIMS, preferred_element_type=f32)
            if last - first < COLS:
                part = jnp.concatenate([part, jnp.zeros((CX, COLS - (last - first)), f32)], axis=1)
                if half == 0:
                    part = part + jnp.concatenate([conv_ref[:, 0:COLS], jnp.zeros((CX - C, COLS), f32)], axis=0)
            pack_ref[half, blk * CX : (blk + 1) * CX, :] = part.astype(bf16)
        pack_ref[half, BLOCKS * CX :, :] = jnp.zeros((HALF - BLOCKS * CX, COLS), bf16)
    core = core_ref[0]
    keep_ref[...] = pack_ref[core]
    send_ref[...] = pack_ref[1 - core]


def back_kernel(
    slot_ref,
    near_ref,
    own_ref,
    north_ref,
    south_ref,
    wet_ref,
    cot_ref,
    kern_ref,
    igrad_ref,
    masks_ref,
    rows_ref,
    conv_ref,
):
    fill_masks(slot_ref, near_ref, masks_ref)
    fill_rows(north_ref, NORTH, rows_ref)
    fill_rows(own_ref, OWN, rows_ref)
    fill_rows(south_ref, SOUTH, rows_ref)

    def conv_step(g, carry):
        at = pl.ds(pl.multiple_of(g * 8, 8), 8)
        rows = {r: rows_ref[r, at, :] for r in range(3 * ROWS)}
        kern = kern_ref[at, :]

        def coef(a, b):
            t = TAPS - 1 - 7 * a - b
            return jnp.broadcast_to(kern[:, t : t + 1], (8, COLS))

        total = conv_group(rows, coef, masks_ref, (NORTH, OWN, SOUTH))
        for i in range(ROWS):
            conv_ref[at, lanes(i)] = total[i]
        return carry

    lax.fori_loop(0, GROUPS, conv_step, 0)
    for r in range(ROWS):
        wet = wet_ref[0:1, lanes(r)]
        og = cot_ref[:, lanes(r)].astype(f32) * wet
        igrad_ref[:, lanes(r)] = (wet * (og + conv_ref[:, lanes(r)])).astype(bf16)


def unpack_kernel(factor, core_ref, mine_ref, other_ref, gin_ref, gout_ref, gkern_ref, *rest):
    *vec_refs, gbias_ref, full_ref = rest
    core = core_ref[0]
    full_ref[core] = mine_ref[...].astype(f32) * factor
    full_ref[1 - core] = other_ref[...].astype(f32) * factor
    for blk in range(BLOCKS):
        begin, end = blk * COLS, min((blk + 1) * COLS, HID)
        gin_ref[:, begin:end] = full_ref[0, blk * CX : blk * CX + C, 0 : end - begin]
        gbias_ref[0:1, begin:end] = full_ref[0, blk * CX + C : blk * CX + C + 1, 0 : end - begin]
        gout_ref[:, begin:end] = full_ref[1, blk * CX : blk * CX + C, 0 : end - begin]
    columns = full_ref[0, (BLOCKS - 1) * CX : (BLOCKS - 1) * CX + C, :].T
    gkern_ref[...] = columns[SMALL:VECTORS, :]
    for s, ref in enumerate(vec_refs):
        ref[...] = columns[VECTORS + s : VECTORS + s + 1, :]


def near(x):
    return pltpu.with_memory_space_constraint(x, pltpu.VMEM)


def hbm(shape, dtype):
    return jax.ShapeDtypeStruct(shape, dtype)


def call(kernel, outs, n_smem, args, scratch=(), time=1.0, limit=8):
    args = list(args[:n_smem]) + [near(x) for x in args[n_smem:]]
    return pl.pallas_call(
        kernel,
        out_shape=outs,
        in_specs=[SMEM] * n_smem + [VMEM] * (len(args) - n_smem),
        out_specs=[VMEM] * len(outs),
        scratch_shapes=[pltpu.VMEM(s, d) for s, d in scratch],
        cost_estimate=pl.CostEstimate(flops=int(time * 1.1e9), bytes_accessed=1000000, transcendentals=0),
        compiler_params=pltpu.CompilerParams(vmem_limit_bytes=limit * MIB),
    )(*args)


TILE_AXES = ("y", "z", "core")
PLANE = ("y", "rep")


def shifted(value, steps):
    count = lax.axis_size(TILE_AXES)
    first, last = max(0, -steps), min(count, count - steps)
    return lax.ppermute(value, TILE_AXES, [(s, s + steps) for s in range(first, last)])


def exchange(value, axes):
    return lax.all_to_all(value, axes, 0, 0, tiled=True)


def fold_kernel(value_ref, copies_ref):
    total = value_ref[0].astype(f32)
    for k in range(1, value_ref.shape[0]):
        total = total + value_ref[k].astype(f32)
    total = total.astype(bf16)
    for k in range(copies_ref.shape[0]):
        copies_ref[k] = total


def fold(value, axes, next_axes):
    count, copies = lax.axis_size(axes), lax.axis_size(next_axes)
    rows = value.shape[0] // count
    (out,) = call(
        fold_kernel,
        [pltpu.VMEM((copies, rows, COLS), bf16)],
        0,
        [value.reshape(count, rows, COLS)],
        limit=4,
    )
    return out.reshape(copies * rows, COLS)


def reduce_pack(keep, send):
    swap = [(0, 1), (1, 0)]
    got = lax.ppermute(send, "core", swap)
    pair = (keep.astype(f32) + got.astype(f32)).astype(bf16)
    part = fold(exchange(pair, PLANE), PLANE, "z")
    part = exchange(part, "z")
    mine = exchange(fold(part, "z", PLANE), PLANE)
    return mine, lax.ppermute(mine, "core", swap)


def step(
    fields,
    wet_bits,
    neighbours,
    kernel,
    conv_bias,
    ln_gain,
    ln_shift,
    in_weight,
    in_bias,
    out_weight,
    out_bias,
    cotangent,
):
    act2 = (C, CELLS)
    slot = lax.axis_index(TILE_AXES).astype(jnp.int32).reshape(1)
    core = lax.axis_index("core").astype(jnp.int32).reshape(1)
    cot = cotangent.reshape(act2)
    masked, wet = call(
        mask_kernel,
        [pltpu.VMEM(act2, bf16), pltpu.VMEM((8, CELLS), f32)],
        1,
        [wet_bits.transpose(2, 0, 1), fields.reshape(act2)],
        limit=4,
    )
    from_north = shifted(masked, 1)
    from_south = shifted(masked, -1)
    chan = jnp.stack([conv_bias, ln_gain, ln_shift, out_bias], axis=1)
    high = lax.reduce_precision(in_bias, 8, 7)
    bias_rows = jnp.stack([high, in_bias - high]).astype(bf16)
    inwt = jnp.concatenate([in_weight, bias_rows, jnp.zeros((CX - C - 2, HID), bf16)], axis=0).T
    chan, inwt = lax.optimization_barrier((chan, inwt))
    masks, coef, chans, part, ograd, agrad, osum = call(
        pre_kernel,
        [
            pltpu.VMEM((21, 8, COLS), f32),
            pltpu.VMEM((TAPS, C, COLS), f32),
            pltpu.VMEM((4, C, COLS), f32),
            pltpu.VMEM(act2, f32),
            pltpu.VMEM((CX, CELLS), bf16),
            pltpu.VMEM((HID, CELLS), f32),
            pltpu.VMEM((C, COLS), f32),
        ],
        2,
        [slot, neighbours, masked, wet, cot, kernel, chan, out_weight],
        [((ROWS, C, COLS), f32)],
        time=6.0,
        limit=8,
    )
    field, cgrad, keep, send = call(
        main_kernel,
        [
            hbm(act2, bf16),
            pltpu.VMEM(act2, bf16),
            pltpu.VMEM((HALF, COLS), bf16),
            pltpu.VMEM((HALF, COLS), bf16),
        ],
        1,
        [
            core,
            masked,
            from_north,
            from_south,
            wet,
            masks,
            coef,
            chans,
            part,
            ograd,
            agrad,
            osum,
            in_weight,
            inwt,
            out_weight.T,
        ],
        [
            ((4 * ROWS, C, COLS), f32),
            (act2, f32),
            ((8, CELLS), f32),
            ((HID, CELLS), f32),
            ((CX, CELLS), bf16),
            ((HID, CELLS), bf16),
            ((HID, CELLS), bf16),
            ((4, C, COLS), f32),
            ((2, HALF, COLS), bf16),
        ],
        time=12.0,
        limit=20,
    )
    cg_north = shifted(cgrad, 1)
    cg_south = shifted(cgrad, -1)
    (input_grad,) = call(
        back_kernel,
        [hbm(act2, bf16)],
        2,
        [slot, neighbours, cgrad, cg_north, cg_south, wet, cot, kernel],
        [((21, 8, COLS), f32), ((3 * ROWS, C, COLS), f32), (act2, f32)],
        time=6.0,
        limit=8,
    )
    mine, other = reduce_pack(keep, send)
    total_cells = lax.axis_size(TILE_AXES) * lax.axis_size("rep") * CELLS
    factor = float(total_cells) ** -0.5
    gin, gout, gkern, gbias, ggain, gshift, gobias, gibias = call(
        lambda *refs: unpack_kernel(factor, *refs),
        [hbm((C, HID), f32), hbm((C, HID), f32), hbm((TAPS, C), f32)] + [hbm((1, C), f32)] * 4 + [hbm((1, HID), f32)],
        1,
        [core, mine, other],
        [((2, HALF, COLS), f32)],
        limit=8,
    )
    return (
        field.reshape(1, 1, C, CELLS),
        input_grad.reshape(1, 1, C, CELLS),
        gkern.T,
        gbias.reshape(C),
        ggain.reshape(C),
        gshift.reshape(C),
        gin,
        gibias.reshape(HID),
        gout.T,
        gobias.reshape(C),
    )


def solution(mesh):
    rep = mesh.shape["rep"]
    fine = Mesh(mesh.devices.reshape(4, -1, 2, rep), ("y", "z", "core", "rep"))
    tile = P("rep", TILE_AXES, None, None)
    placed = (tile, P(TILE_AXES, None, None), P(TILE_AXES, None)) + (P(),) * 8 + (tile,)
    return jax.shard_map(
        step,
        mesh=fine,
        in_specs=placed,
        out_specs=(tile, tile) + (P(),) * 8,
        check_vma=False,
    )
```

```python
import jax
import jax.numpy as jnp
from jax import lax
from jax.experimental import pallas as pl
from jax.experimental.pallas import tpu as pltpu
from jax.sharding import Mesh, PartitionSpec as P


C = 200
CX = 208
HID = 800
ROWS = 6
COLS = 128
CELLS = 768
WORDS = 5
BITS = 30
TAPS = 49
GROUPS = C // 8
BLOCKS = 7
HALF = 1536
SMALL = BLOCKS * CX
PAIRS = 27
MIB = 1 << 20
UNROLL = 5

bf16 = jnp.bfloat16
f32 = jnp.float32
gelu_scale = 0.7978845608028654
VMEM = pl.BlockSpec(memory_space=pltpu.VMEM)
SMEM = pl.BlockSpec(memory_space=pltpu.SMEM)
NT_DIMS = (((1,), (1,)), ((), ()))
NORTH, OWN, SOUTH = 0, 1, 2


def row_class(row):
    return row // ROWS


def lanes(r):
    return slice(r * COLS, (r + 1) * COLS)


def wet_row(bits_ref, r):
    col = lax.broadcasted_iota(jnp.int32, (8, COLS), 1)
    word = jnp.zeros((8, COLS), jnp.int32)
    shift = col
    for w in range(WORDS):
        word = jnp.where(col >= BITS * w, bits_ref[w, 0, r], word)
        shift = jnp.where(col >= BITS * w, col - BITS * w, shift)
    return jnp.bitwise_and(jnp.right_shift(word, shift), 1).astype(f32)


def mask_kernel(bits_ref, fields_ref, masked_ref, wet_ref):
    for r in range(ROWS):
        wet = wet_row(bits_ref, r)
        wet_ref[:, lanes(r)] = wet
        masked_ref[:, lanes(r)] = (fields_ref[:, lanes(r)].astype(f32) * wet[0:1]).astype(bf16)


def fill_masks(slot_ref, near_ref, masks_ref):
    slot = slot_ref[0]

    def flag(k, step):
        return jnp.where(near_ref[0, k] == slot + step, 1.0, 0.0).astype(f32)

    lane = lax.broadcasted_iota(jnp.int32, (8, COLS), 1)
    triples = (
        (flag(0, -1), flag(4, -1), flag(5, -1)),
        (jnp.float32(1.0), flag(2, 0), flag(3, 0)),
        (flag(1, 1), flag(6, 1), flag(7, 1)),
    )
    for cls, (centre, west, east) in enumerate(triples):
        for b in range(7):
            off = 2 * b - 6
            mask = jnp.full((8, COLS), centre, f32)
            if off > 0:
                mask = jnp.where(lane < off, jnp.full((8, COLS), east, f32), mask)
            if off < 0:
                mask = jnp.where(lane >= COLS + off, jnp.full((8, COLS), west, f32), mask)
            masks_ref[7 * cls + b] = mask


def fill_rows(ref, part, rows_ref):
    for r in range(ROWS):
        rows_ref[ROWS * part + r] = ref[:, lanes(r)].astype(f32)


def conv_group(rows, coef, masks_ref, classes):
    total = [None] * ROWS
    for b in range(7):
        off = 2 * b - 6
        masked = {}
        for r in rows:
            plain = b == 3 and row_class(r) == OWN
            masked[r] = rows[r] if plain else rows[r] * masks_ref[7 * row_class(r) + b]
        taps = [coef(a, b) for a in range(7)]
        for i in range(ROWS):
            acc = None
            for a in range(7):
                if row_class(i + 2 * a) in classes:
                    term = taps[a] * masked[i + 2 * a]
                    acc = term if acc is None else acc + term
            if off != 0:
                acc = pltpu.roll(acc, (-off) % COLS, 1)
            total[i] = acc if total[i] is None else total[i] + acc
    return total


def fill_coef(table_ref, coef_ref):
    for t in range(TAPS):
        coef_ref[t] = jnp.broadcast_to(table_ref[:, t : t + 1], (C, COLS))


def pre_kernel(
    slot_ref,
    near_ref,
    own_ref,
    wet_ref,
    cot_ref,
    table_ref,
    outw_ref,
    masks_ref,
    coef_ref,
    chans_ref,
    part_ref,
    ograd_ref,
    agrad_ref,
    osum_ref,
    rows_ref,
):
    fill_masks(slot_ref, near_ref, masks_ref)
    fill_rows(own_ref, 0, rows_ref)
    osum = jnp.zeros((C, COLS), f32)
    for r in range(ROWS):
        og = cot_ref[:, lanes(r)].astype(f32) * wet_ref[0:1, lanes(r)]
        osum = osum + og
        ograd_ref[:, lanes(r)] = jnp.concatenate([og, jnp.zeros((CX - C, COLS), f32)], axis=0).astype(bf16)
    osum_ref[...] = osum
    agrad_ref[...] = jnp.dot(outw_ref[...], ograd_ref[0:C, :], preferred_element_type=f32)
    fill_coef(table_ref, coef_ref)
    for k in range(4):
        chans_ref[k] = jnp.broadcast_to(table_ref[:, TAPS + k : TAPS + k + 1], (C, COLS))

    def step(g, carry):
        at = pl.ds(pl.multiple_of(g * 8, 8), 8)
        rows = {ROWS + r: rows_ref[r, at, :] for r in range(ROWS)}
        total = conv_group(rows, lambda a, b: coef_ref[7 * a + b, at, :], masks_ref, (OWN,))
        for i in range(ROWS):
            part_ref[at, lanes(i)] = total[i] + chans_ref[0, at, :]
        return carry

    lax.fori_loop(0, GROUPS, step, 0, unroll=UNROLL)


def main_kernel(
    core_ref,
    own_ref,
    north_ref,
    south_ref,
    masks_ref,
    coef_ref,
    chans_ref,
    part_ref,
    ograd_ref,
    agrad_ref,
    osum_ref,
    inw_ref,
    inwt_ref,
    cgrad_ref,
    act_ref,
    keep_ref,
    send_ref,
    rows_ref,
    conv_ref,
    istd_ref,
    hid_ref,
    norm_ref,
    hgrad_ref,
    sums_ref,
    small_ref,
    pack_ref,
):
    fill_rows(north_ref, NORTH, rows_ref)
    fill_rows(own_ref, OWN, rows_ref)
    fill_rows(south_ref, SOUTH, rows_ref)

    def conv_step(g, carry):
        at = pl.ds(pl.multiple_of(g * 8, 8), 8)
        rows = {r: rows_ref[r, at, :] for r in range(3 * ROWS) if row_class(r) != OWN}
        total = conv_group(rows, lambda a, b: coef_ref[7 * a + b, at, :], masks_ref, (NORTH, SOUTH))
        for i in range(ROWS):
            conv_ref[at, lanes(i)] = total[i] + part_ref[at, lanes(i)]
        return carry

    lax.fori_loop(0, GROUPS, conv_step, 0, unroll=UNROLL)

    extra = lax.broadcasted_iota(jnp.int32, (8, COLS), 0)
    extra = jnp.where(extra < 2, 1.0, 0.0).astype(f32)
    for r in range(ROWS):
        x = conv_ref[:, lanes(r)]
        mean = jnp.sum(x, axis=0, keepdims=True) * (1.0 / C)
        x = x - mean
        var = jnp.sum(x * x, axis=0, keepdims=True) * (1.0 / C)
        istd = lax.rsqrt(var + 1e-06)
        normed = x * istd
        conv_ref[:, lanes(r)] = normed
        istd_ref[:, lanes(r)] = jnp.broadcast_to(istd, (8, COLS))
        no = jnp.concatenate([normed * chans_ref[1] + chans_ref[2], extra], axis=0)
        norm_ref[:, lanes(r)] = no.astype(bf16)

    hid_ref[...] = jnp.dot(inwt_ref[...], norm_ref[...], preferred_element_type=f32)

    def gelu_step(i, carry):
        at = pl.ds(pl.multiple_of(i * 16, 16), 16)
        h = hid_ref[at, :]
        h2 = h * h
        t = jnp.tanh(h * (gelu_scale + (gelu_scale * 0.044715) * h2))
        half = 0.5 + 0.5 * t
        act_ref[at, :] = (h * half).astype(bf16)
        slope = (0.5 * gelu_scale) + (0.5 * gelu_scale * 3.0 * 0.044715) * h2
        deriv = half + h * (1.0 - t * t) * slope
        hgrad_ref[at, :] = (agrad_ref[at, :] * deriv).astype(bf16)
        return carry

    lax.fori_loop(0, HID // 16, gelu_step, 0, unroll=2)

    hid_ref[0:C, :] = jnp.dot(inw_ref[...], hgrad_ref[...], preferred_element_type=f32)
    gsum = jnp.zeros((C, COLS), f32)
    ssum = jnp.zeros((C, COLS), f32)
    bsum = jnp.zeros((C, COLS), f32)
    cg_base = 3 * ROWS
    for r in range(ROWS):
        ng = hid_ref[0:C, lanes(r)]
        normed = conv_ref[:, lanes(r)]
        ssum = ssum + ng
        gsum = gsum + ng * normed
        scaled = ng * chans_ref[1]
        m1 = jnp.sum(scaled, axis=0, keepdims=True) * (1.0 / C)
        m2 = jnp.sum(scaled * normed, axis=0, keepdims=True) * (1.0 / C)
        cg = (istd_ref[0:1, lanes(r)] * (scaled - m1 - normed * m2)).astype(bf16)
        cgrad_ref[:, lanes(r)] = cg
        rows_ref[cg_base + r] = cg.astype(f32)
        bsum = bsum + cg.astype(f32)
    for s, vec in enumerate((bsum, gsum, ssum, osum_ref[...], jnp.zeros((C, COLS), f32))):
        sums_ref[(TAPS + s) // 2, :, lanes((TAPS + s) % 2)] = vec.astype(bf16)

    def tap_step(g, carry):
        at = pl.ds(pl.multiple_of(g * 8, 8), 8)
        for b in range(7):
            off = 2 * b - 6
            acc = [None] * 7
            for i in range(ROWS):
                turned = rows_ref[cg_base + i, at, :]
                if off != 0:
                    turned = pltpu.roll(turned, off % COLS, 1)
                parts = [turned if b == 3 and cls == OWN else turned * masks_ref[7 * cls + b] for cls in range(3)]
                for a in range(7):
                    r = i + 2 * a
                    term = parts[row_class(r)] * rows_ref[r, at, :]
                    acc[a] = term if acc[a] is None else acc[a] + term
            for a in range(7):
                t = 7 * a + b
                sums_ref[t // 2, at, lanes(t % 2)] = acc[a].astype(bf16)
        return carry

    lax.fori_loop(0, GROUPS, tap_step, 0, unroll=UNROLL)
    lane = lax.broadcasted_iota(jnp.int32, (8, 2 * COLS), 1)
    line = lax.broadcasted_iota(jnp.int32, (8, 2 * COLS), 0)
    pick = jnp.where((lane >= COLS) == (line == 1), jnp.where(line < 2, 1.0, 0.0), 0.0).astype(bf16)
    small_ref[...] = jnp.zeros(small_ref.shape, f32)
    for k in range(PAIRS):
        both = lax.dot_general(pick, sums_ref[k], NT_DIMS, preferred_element_type=f32)
        small_ref[2 * k : 2 * k + 2, 0:C] = both[0:2, :]

    for half, (left_ref, right_ref) in enumerate(((norm_ref, hgrad_ref), (ograd_ref, act_ref))):
        for first in range(0, HID, 2 * COLS):
            last = min(first + 2 * COLS, HID)
            blk = first // COLS
            part = lax.dot_general(left_ref[...], right_ref[first:last, :], NT_DIMS, preferred_element_type=f32)
            if last - first < COLS:
                part = jnp.concatenate([part, jnp.zeros((CX, COLS - (last - first)), f32)], axis=1)
            pack_ref[half, blk * CX : (blk + 1) * CX, :] = part[:, 0:COLS].astype(bf16)
            if last - first > COLS:
                pack_ref[half, (blk + 1) * CX : (blk + 2) * CX, :] = part[:, COLS:].astype(bf16)
        pack_ref[half, SMALL : SMALL + 2 * PAIRS + 2, :] = small_ref[:, lanes(half)].astype(bf16)
        pack_ref[half, SMALL + 2 * PAIRS + 2 :, :] = jnp.zeros((HALF - SMALL - 2 * PAIRS - 2, COLS), bf16)
    core = core_ref[0]
    keep_ref[...] = pack_ref[core]
    send_ref[...] = pack_ref[1 - core]


def field_kernel(own_ref, wet_ref, table_ref, act_ref, outwt_ref, field_ref, hid_ref):
    hid_ref[...] = jnp.dot(outwt_ref[...], act_ref[...], preferred_element_type=f32)
    bias = jnp.broadcast_to(table_ref[:, TAPS + 3 : TAPS + 4], (C, COLS))
    for r in range(ROWS):
        update = hid_ref[:, lanes(r)] + bias
        own = own_ref[:, lanes(r)].astype(f32)
        field_ref[:, lanes(r)] = (wet_ref[0:1, lanes(r)] * (own + update)).astype(bf16)


def back_kernel(
    slot_ref,
    near_ref,
    own_ref,
    north_ref,
    south_ref,
    wet_ref,
    cot_ref,
    table_ref,
    igrad_ref,
    masks_ref,
    rows_ref,
    conv_ref,
    coef_ref,
):
    fill_masks(slot_ref, near_ref, masks_ref)
    fill_coef(table_ref, coef_ref)
    fill_rows(north_ref, NORTH, rows_ref)
    fill_rows(own_ref, OWN, rows_ref)
    fill_rows(south_ref, SOUTH, rows_ref)

    def conv_step(g, carry):
        at = pl.ds(pl.multiple_of(g * 8, 8), 8)
        rows = {r: rows_ref[r, at, :] for r in range(3 * ROWS)}
        total = conv_group(
            rows, lambda a, b: coef_ref[TAPS - 1 - 7 * a - b, at, :], masks_ref, (NORTH, OWN, SOUTH)
        )
        for i in range(ROWS):
            conv_ref[at, lanes(i)] = total[i]
        return carry

    lax.fori_loop(0, GROUPS, conv_step, 0, unroll=UNROLL)
    for r in range(ROWS):
        wet = wet_ref[0:1, lanes(r)]
        og = cot_ref[:, lanes(r)].astype(f32) * wet
        igrad_ref[:, lanes(r)] = (wet * (og + conv_ref[:, lanes(r)])).astype(bf16)


def unpack_kernel(factor, core_ref, mine_ref, other_ref, gin_ref, gout_ref, gkern_ref, *rest):
    *vec_refs, gbias_ref, full_ref = rest
    core = core_ref[0]
    full_ref[core] = mine_ref[...].astype(f32) * factor
    full_ref[1 - core] = other_ref[...].astype(f32) * factor
    for blk in range(BLOCKS):
        begin, end = blk * COLS, min((blk + 1) * COLS, HID)
        gin_ref[:, begin:end] = full_ref[0, blk * CX : blk * CX + C, 0 : end - begin]
        gbias_ref[0:1, begin:end] = full_ref[0, blk * CX + C : blk * CX + C + 1, 0 : end - begin]
        gout_ref[:, begin:end] = full_ref[1, blk * CX : blk * CX + C, 0 : end - begin]
    for half, begin, end in ((0, 0, COLS), (1, COLS, C)):
        small = full_ref[half, SMALL : SMALL + 2 * PAIRS + 2, 0 : end - begin]
        gkern_ref[:, begin:end] = small[0:TAPS]
        for s, ref in enumerate(vec_refs):
            ref[:, begin:end] = small[TAPS + s : TAPS + s + 1]


def near(x):
    return pltpu.with_memory_space_constraint(x, pltpu.VMEM)


def hbm(shape, dtype):
    return jax.ShapeDtypeStruct(shape, dtype)


def call(kernel, outs, n_smem, args, scratch=(), time=1.0, limit=8):
    args = list(args[:n_smem]) + [near(x) for x in args[n_smem:]]
    return pl.pallas_call(
        kernel,
        out_shape=outs,
        in_specs=[SMEM] * n_smem + [VMEM] * (len(args) - n_smem),
        out_specs=[VMEM] * len(outs),
        scratch_shapes=[pltpu.VMEM(s, d) for s, d in scratch],
        cost_estimate=pl.CostEstimate(flops=int(time * 1.1e9), bytes_accessed=1000000, transcendentals=0),
        compiler_params=pltpu.CompilerParams(vmem_limit_bytes=limit * MIB),
    )(*args)


TILE_AXES = ("y", "z", "core")
PLANE = ("y", "rep")


def shifted(value, steps):
    count = lax.axis_size(TILE_AXES)
    first, last = max(0, -steps), min(count, count - steps)
    return lax.ppermute(value, TILE_AXES, [(s, s + steps) for s in range(first, last)])


def exchange(value, axes):
    return lax.all_to_all(value, axes, 0, 0, tiled=True)


def add_kernel(keep_ref, got_ref, pair_ref):
    pair_ref[...] = (keep_ref[...].astype(f32) + got_ref[...].astype(f32)).astype(bf16)


def fold_kernel(value_ref, copies_ref):
    total = value_ref[0].astype(f32)
    for k in range(1, value_ref.shape[0]):
        total = total + value_ref[k].astype(f32)
    total = total.astype(bf16)
    for k in range(copies_ref.shape[0]):
        copies_ref[k] = total


def fold(value, axes, next_axes):
    count, copies = lax.axis_size(axes), lax.axis_size(next_axes)
    rows = value.shape[0] // count
    (out,) = call(
        fold_kernel,
        [pltpu.VMEM((copies, rows, COLS), bf16)],
        0,
        [value.reshape(count, rows, COLS)],
        limit=4,
    )
    return out.reshape(copies * rows, COLS)


def reduce_pack(keep, send):
    swap = [(0, 1), (1, 0)]
    got = lax.ppermute(send, "core", swap)
    (pair,) = call(add_kernel, [pltpu.VMEM((HALF, COLS), bf16)], 0, [keep, got], limit=4)
    part = exchange(pair, PLANE)
    part = fold(part, PLANE, "z")
    part = exchange(part, "z")
    mine = exchange(fold(part, "z", PLANE), PLANE)
    return mine, lax.ppermute(mine, "core", swap)


def step(
    fields,
    wet_bits,
    neighbours,
    kernel,
    conv_bias,
    ln_gain,
    ln_shift,
    in_weight,
    in_bias,
    out_weight,
    out_bias,
    cotangent,
):
    act2 = (C, CELLS)
    slot = lax.axis_index(TILE_AXES).astype(jnp.int32).reshape(1)
    core = lax.axis_index("core").astype(jnp.int32).reshape(1)
    cot = cotangent.reshape(act2)
    masked, wet = call(
        mask_kernel,
        [pltpu.VMEM(act2, bf16), pltpu.VMEM((8, CELLS), f32)],
        1,
        [wet_bits.transpose(2, 0, 1), fields.reshape(act2)],
        limit=4,
    )
    from_north = shifted(masked, 1)
    from_south = shifted(masked, -1)
    vectors = jnp.stack([conv_bias, ln_gain, ln_shift, out_bias])
    table = jnp.concatenate([kernel.T, vectors], axis=0).T
    high = lax.reduce_precision(in_bias, 8, 7)
    bias_rows = jnp.stack([high, in_bias - high]).astype(bf16)
    inwt = jnp.concatenate([in_weight, bias_rows, jnp.zeros((CX - C - 2, HID), bf16)], axis=0).T
    table, inwt = lax.optimization_barrier((table, inwt))
    masks, coef, chans, part, ograd, agrad, osum = call(
        pre_kernel,
        [
            pltpu.VMEM((21, 8, COLS), f32),
            pltpu.VMEM((TAPS, C, COLS), f32),
            pltpu.VMEM((4, C, COLS), f32),
            pltpu.VMEM(act2, f32),
            pltpu.VMEM((CX, CELLS), bf16),
            pltpu.VMEM((HID, CELLS), f32),
            pltpu.VMEM((C, COLS), f32),
        ],
        2,
        [slot, neighbours, masked, wet, cot, table, out_weight],
        [((ROWS, C, COLS), f32)],
        time=6.0,
        limit=8,
    )
    cgrad, act, keep, send = call(
        main_kernel,
        [
            pltpu.VMEM(act2, bf16),
            pltpu.VMEM((HID, CELLS), bf16),
            pltpu.VMEM((HALF, COLS), bf16),
            pltpu.VMEM((HALF, COLS), bf16),
        ],
        1,
        [
            core,
            masked,
            from_north,
            from_south,
            masks,
            coef,
            chans,
            part,
            ograd,
            agrad,
            osum,
            in_weight,
            inwt,
        ],
        [
            ((4 * ROWS, C, COLS), f32),
            (act2, f32),
            ((8, CELLS), f32),
            ((HID, CELLS), f32),
            ((CX, CELLS), bf16),
            ((HID, CELLS), bf16),
            ((PAIRS, C, 2 * COLS), bf16),
            ((2 * PAIRS + 2, 2 * COLS), f32),
            ((2, HALF, COLS), bf16),
        ],
        time=12.0,
        limit=24,
    )
    cg_north = shifted(cgrad, 1)
    cg_south = shifted(cgrad, -1)
    (field,) = call(
        field_kernel,
        [hbm(act2, bf16)],
        0,
        [masked, wet, table, act, out_weight.T],
        [(act2, f32)],
        time=1.5,
        limit=4,
    )
    (input_grad,) = call(
        back_kernel,
        [hbm(act2, bf16)],
        2,
        [slot, neighbours, cgrad, cg_north, cg_south, wet, cot, table],
        [((21, 8, COLS), f32), ((3 * ROWS, C, COLS), f32), (act2, f32), ((TAPS, C, COLS), f32)],
        time=6.0,
        limit=14,
    )
    mine, other = reduce_pack(keep, send)
    total_cells = lax.axis_size(TILE_AXES) * lax.axis_size("rep") * CELLS
    factor = float(total_cells) ** -0.5
    gin, gout, gkern, gbias, ggain, gshift, gobias, gibias = call(
        lambda *refs: unpack_kernel(factor, *refs),
        [hbm((C, HID), f32), hbm((C, HID), f32), hbm((TAPS, C), f32)] + [hbm((1, C), f32)] * 4 + [hbm((1, HID), f32)],
        1,
        [core, mine, other],
        [((2, HALF, COLS), f32)],
        limit=8,
    )
    return (
        field.reshape(1, 1, C, CELLS),
        input_grad.reshape(1, 1, C, CELLS),
        gkern.T,
        gbias.reshape(C),
        ggain.reshape(C),
        gshift.reshape(C),
        gin,
        gibias.reshape(HID),
        gout.T,
        gobias.reshape(C),
    )


def solution(mesh):
    rep = mesh.shape["rep"]
    fine = Mesh(mesh.devices.reshape(4, -1, 2, rep), ("y", "z", "core", "rep"))
    tile = P("rep", TILE_AXES, None, None)
    placed = (tile, P(TILE_AXES, None, None), P(TILE_AXES, None)) + (P(),) * 8 + (tile,)
    return jax.shard_map(
        step,
        mesh=fine,
        in_specs=placed,
        out_specs=(tile, tile) + (P(),) * 8,
        check_vma=False,
    )
```

```python
import jax
import jax.numpy as jnp
from jax import lax
from jax.experimental import pallas as pl
from jax.experimental.pallas import tpu as pltpu
from jax.sharding import Mesh, PartitionSpec as P


C = 200
CX = 208
HID = 800
ROWS = 6
COLS = 128
CELLS = 768
WORDS = 5
BITS = 30
TAPS = 49
GROUPS = C // 8
BLOCKS = 7
HALF = 1536
SMALL = BLOCKS * CX
PAIRS = 27
MIB = 1 << 20
UNROLL = 5

bf16 = jnp.bfloat16
f32 = jnp.float32
gelu_scale = 0.7978845608028654
VMEM = pl.BlockSpec(memory_space=pltpu.VMEM)
SMEM = pl.BlockSpec(memory_space=pltpu.SMEM)
NT_DIMS = (((1,), (1,)), ((), ()))
NORTH, OWN, SOUTH = 0, 1, 2


def row_class(row):
    return row // ROWS


def lanes(r):
    return slice(r * COLS, (r + 1) * COLS)


def wet_row(bits_ref, r):
    col = lax.broadcasted_iota(jnp.int32, (8, COLS), 1)
    word = jnp.zeros((8, COLS), jnp.int32)
    shift = col
    for w in range(WORDS):
        word = jnp.where(col >= BITS * w, bits_ref[w, 0, r], word)
        shift = jnp.where(col >= BITS * w, col - BITS * w, shift)
    return jnp.bitwise_and(jnp.right_shift(word, shift), 1).astype(f32)


def mask_kernel(bits_ref, fields_ref, masked_ref, wet_ref):
    for r in range(ROWS):
        wet = wet_row(bits_ref, r)
        wet_ref[:, lanes(r)] = wet
        masked_ref[:, lanes(r)] = (fields_ref[:, lanes(r)].astype(f32) * wet[0:1]).astype(bf16)


def fill_masks(slot_ref, near_ref, masks_ref):
    slot = slot_ref[0]

    def flag(k, step):
        return jnp.where(near_ref[0, k] == slot + step, 1.0, 0.0).astype(f32)

    lane = lax.broadcasted_iota(jnp.int32, (8, COLS), 1)
    triples = (
        (flag(0, -1), flag(4, -1), flag(5, -1)),
        (jnp.float32(1.0), flag(2, 0), flag(3, 0)),
        (flag(1, 1), flag(6, 1), flag(7, 1)),
    )
    for cls, (centre, west, east) in enumerate(triples):
        for b in range(7):
            off = 2 * b - 6
            mask = jnp.full((8, COLS), centre, f32)
            if off > 0:
                mask = jnp.where(lane < off, jnp.full((8, COLS), east, f32), mask)
            if off < 0:
                mask = jnp.where(lane >= COLS + off, jnp.full((8, COLS), west, f32), mask)
            masks_ref[7 * cls + b] = mask


def fill_rows(ref, part, rows_ref):
    for r in range(ROWS):
        rows_ref[ROWS * part + r] = ref[:, lanes(r)].astype(f32)


def conv_group(rows, coef, masks_ref, classes):
    total = [None] * ROWS
    for b in range(7):
        off = 2 * b - 6
        masked = {}
        for r in rows:
            plain = b == 3 and row_class(r) == OWN
            masked[r] = rows[r] if plain else rows[r] * masks_ref[7 * row_class(r) + b]
        taps = [coef(a, b) for a in range(7)]
        for i in range(ROWS):
            acc = None
            for a in range(7):
                if row_class(i + 2 * a) in classes:
                    term = taps[a] * masked[i + 2 * a]
                    acc = term if acc is None else acc + term
            if off != 0:
                acc = pltpu.roll(acc, (-off) % COLS, 1)
            total[i] = acc if total[i] is None else total[i] + acc
    return total


def fill_coef(table_ref, coef_ref):
    for t in range(TAPS):
        coef_ref[t] = jnp.broadcast_to(table_ref[:, t : t + 1], (C, COLS))


def pre_kernel(
    slot_ref,
    near_ref,
    own_ref,
    wet_ref,
    cot_ref,
    kern_ref,
    vec0_ref,
    vec1_ref,
    vec2_ref,
    vec3_ref,
    outw_ref,
    table_ref,
    masks_ref,
    coef_ref,
    chans_ref,
    part_ref,
    ograd_ref,
    agrad_ref,
    osum_ref,
    rows_ref,
    flat_ref,
):
    flat_ref[...] = jnp.zeros(flat_ref.shape, f32)
    flat_ref[0:TAPS, 0:C] = kern_ref[...]
    for k, vec_ref in enumerate((vec0_ref, vec1_ref, vec2_ref, vec3_ref)):
        flat_ref[TAPS + k : TAPS + k + 1, 0:C] = vec_ref[...]
    table_ref[0:COLS, :] = flat_ref[:, 0:COLS].T
    table_ref[COLS:C, :] = flat_ref[:, COLS:].T[0 : C - COLS, :]
    fill_masks(slot_ref, near_ref, masks_ref)
    fill_rows(own_ref, 0, rows_ref)
    osum = jnp.zeros((C, COLS), f32)
    for r in range(ROWS):
        og = cot_ref[:, lanes(r)].astype(f32) * wet_ref[0:1, lanes(r)]
        osum = osum + og
        ograd_ref[:, lanes(r)] = jnp.concatenate([og, jnp.zeros((CX - C, COLS), f32)], axis=0).astype(bf16)
    osum_ref[...] = osum
    agrad_ref[...] = jnp.dot(outw_ref[...], ograd_ref[0:C, :], preferred_element_type=f32)
    fill_coef(table_ref, coef_ref)
    for k in range(4):
        chans_ref[k] = jnp.broadcast_to(table_ref[:, TAPS + k : TAPS + k + 1], (C, COLS))

    def step(g, carry):
        at = pl.ds(pl.multiple_of(g * 8, 8), 8)
        rows = {ROWS + r: rows_ref[r, at, :] for r in range(ROWS)}
        total = conv_group(rows, lambda a, b: coef_ref[7 * a + b, at, :], masks_ref, (OWN,))
        for i in range(ROWS):
            part_ref[at, lanes(i)] = total[i] + chans_ref[0, at, :]
        return carry

    lax.fori_loop(0, GROUPS, step, 0, unroll=UNROLL)


def main_kernel(
    core_ref,
    own_ref,
    north_ref,
    south_ref,
    masks_ref,
    coef_ref,
    chans_ref,
    part_ref,
    ograd_ref,
    agrad_ref,
    osum_ref,
    inw_ref,
    inwt_ref,
    cgrad_ref,
    act_ref,
    keep_ref,
    send_ref,
    rows_ref,
    conv_ref,
    istd_ref,
    hid_ref,
    norm_ref,
    hgrad_ref,
    sums_ref,
    small_ref,
    pack_ref,
):
    fill_rows(north_ref, NORTH, rows_ref)
    fill_rows(own_ref, OWN, rows_ref)
    fill_rows(south_ref, SOUTH, rows_ref)

    def conv_step(g, carry):
        at = pl.ds(pl.multiple_of(g * 8, 8), 8)
        rows = {r: rows_ref[r, at, :] for r in range(3 * ROWS) if row_class(r) != OWN}
        total = conv_group(rows, lambda a, b: coef_ref[7 * a + b, at, :], masks_ref, (NORTH, SOUTH))
        for i in range(ROWS):
            conv_ref[at, lanes(i)] = total[i] + part_ref[at, lanes(i)]
        return carry

    lax.fori_loop(0, GROUPS, conv_step, 0, unroll=UNROLL)

    extra = lax.broadcasted_iota(jnp.int32, (8, COLS), 0)
    extra = jnp.where(extra < 2, 1.0, 0.0).astype(f32)
    for r in range(ROWS):
        x = conv_ref[:, lanes(r)]
        mean = jnp.sum(x, axis=0, keepdims=True) * (1.0 / C)
        x = x - mean
        var = jnp.sum(x * x, axis=0, keepdims=True) * (1.0 / C)
        istd = lax.rsqrt(var + 1e-06)
        normed = x * istd
        conv_ref[:, lanes(r)] = normed
        istd_ref[:, lanes(r)] = jnp.broadcast_to(istd, (8, COLS))
        no = jnp.concatenate([normed * chans_ref[1] + chans_ref[2], extra], axis=0)
        norm_ref[:, lanes(r)] = no.astype(bf16)

    hid_ref[...] = jnp.dot(inwt_ref[...], norm_ref[...], preferred_element_type=f32)

    def gelu_step(i, carry):
        at = pl.ds(pl.multiple_of(i * 16, 16), 16)
        h = hid_ref[at, :]
        h2 = h * h
        t = jnp.tanh(h * (gelu_scale + (gelu_scale * 0.044715) * h2))
        half = 0.5 + 0.5 * t
        act_ref[at, :] = (h * half).astype(bf16)
        slope = (0.5 * gelu_scale) + (0.5 * gelu_scale * 3.0 * 0.044715) * h2
        deriv = half + h * (1.0 - t * t) * slope
        hgrad_ref[at, :] = (agrad_ref[at, :] * deriv).astype(bf16)
        return carry

    lax.fori_loop(0, HID // 16, gelu_step, 0, unroll=2)

    hid_ref[0:C, :] = jnp.dot(inw_ref[...], hgrad_ref[...], preferred_element_type=f32)
    gsum = jnp.zeros((C, COLS), f32)
    ssum = jnp.zeros((C, COLS), f32)
    bsum = jnp.zeros((C, COLS), f32)
    cg_base = 3 * ROWS
    for r in range(ROWS):
        ng = hid_ref[0:C, lanes(r)]
        normed = conv_ref[:, lanes(r)]
        ssum = ssum + ng
        gsum = gsum + ng * normed
        scaled = ng * chans_ref[1]
        m1 = jnp.sum(scaled, axis=0, keepdims=True) * (1.0 / C)
        m2 = jnp.sum(scaled * normed, axis=0, keepdims=True) * (1.0 / C)
        cg = (istd_ref[0:1, lanes(r)] * (scaled - m1 - normed * m2)).astype(bf16)
        cgrad_ref[:, lanes(r)] = cg
        rows_ref[cg_base + r] = cg.astype(f32)
        bsum = bsum + cg.astype(f32)
    for s, vec in enumerate((bsum, gsum, ssum, osum_ref[...], jnp.zeros((C, COLS), f32))):
        sums_ref[(TAPS + s) // 2, :, lanes((TAPS + s) % 2)] = vec.astype(bf16)

    def tap_step(g, carry):
        at = pl.ds(pl.multiple_of(g * 8, 8), 8)
        for b in range(7):
            off = 2 * b - 6
            acc = [None] * 7
            for i in range(ROWS):
                turned = rows_ref[cg_base + i, at, :]
                if off != 0:
                    turned = pltpu.roll(turned, off % COLS, 1)
                parts = [turned if b == 3 and cls == OWN else turned * masks_ref[7 * cls + b] for cls in range(3)]
                for a in range(7):
                    r = i + 2 * a
                    term = parts[row_class(r)] * rows_ref[r, at, :]
                    acc[a] = term if acc[a] is None else acc[a] + term
            for a in range(7):
                t = 7 * a + b
                sums_ref[t // 2, at, lanes(t % 2)] = acc[a].astype(bf16)
        return carry

    lax.fori_loop(0, GROUPS, tap_step, 0, unroll=UNROLL)
    lane = lax.broadcasted_iota(jnp.int32, (8, 2 * COLS), 1)
    line = lax.broadcasted_iota(jnp.int32, (8, 2 * COLS), 0)
    pick = jnp.where((lane >= COLS) == (line == 1), jnp.where(line < 2, 1.0, 0.0), 0.0).astype(bf16)
    small_ref[...] = jnp.zeros(small_ref.shape, f32)
    for k in range(PAIRS):
        both = lax.dot_general(pick, sums_ref[k], NT_DIMS, preferred_element_type=f32)
        small_ref[2 * k : 2 * k + 2, 0:C] = both[0:2, :]

    for half, (left_ref, right_ref) in enumerate(((norm_ref, hgrad_ref), (ograd_ref, act_ref))):
        for first in range(0, HID, 2 * COLS):
            last = min(first + 2 * COLS, HID)
            blk = first // COLS
            part = lax.dot_general(left_ref[...], right_ref[first:last, :], NT_DIMS, preferred_element_type=f32)
            if last - first < COLS:
                part = jnp.concatenate([part, jnp.zeros((CX, COLS - (last - first)), f32)], axis=1)
            pack_ref[half, blk * CX : (blk + 1) * CX, :] = part[:, 0:COLS].astype(bf16)
            if last - first > COLS:
                pack_ref[half, (blk + 1) * CX : (blk + 2) * CX, :] = part[:, COLS:].astype(bf16)
        pack_ref[half, SMALL : SMALL + 2 * PAIRS + 2, :] = small_ref[:, lanes(half)].astype(bf16)
        pack_ref[half, SMALL + 2 * PAIRS + 2 :, :] = jnp.zeros((HALF - SMALL - 2 * PAIRS - 2, COLS), bf16)
    core = core_ref[0]
    keep_ref[...] = pack_ref[core]
    send_ref[...] = pack_ref[1 - core]


def field_kernel(own_ref, wet_ref, table_ref, act_ref, outwt_ref, field_ref, hid_ref):
    hid_ref[...] = jnp.dot(outwt_ref[...], act_ref[...], preferred_element_type=f32)
    bias = jnp.broadcast_to(table_ref[:, TAPS + 3 : TAPS + 4], (C, COLS))
    for r in range(ROWS):
        update = hid_ref[:, lanes(r)] + bias
        own = own_ref[:, lanes(r)].astype(f32)
        field_ref[:, lanes(r)] = (wet_ref[0:1, lanes(r)] * (own + update)).astype(bf16)


def back_kernel(
    slot_ref,
    near_ref,
    own_ref,
    north_ref,
    south_ref,
    wet_ref,
    cot_ref,
    table_ref,
    igrad_ref,
    masks_ref,
    rows_ref,
    conv_ref,
    coef_ref,
):
    fill_masks(slot_ref, near_ref, masks_ref)
    fill_coef(table_ref, coef_ref)
    fill_rows(north_ref, NORTH, rows_ref)
    fill_rows(own_ref, OWN, rows_ref)
    fill_rows(south_ref, SOUTH, rows_ref)

    def conv_step(g, carry):
        at = pl.ds(pl.multiple_of(g * 8, 8), 8)
        rows = {r: rows_ref[r, at, :] for r in range(3 * ROWS)}
        total = conv_group(
            rows, lambda a, b: coef_ref[TAPS - 1 - 7 * a - b, at, :], masks_ref, (NORTH, OWN, SOUTH)
        )
        for i in range(ROWS):
            conv_ref[at, lanes(i)] = total[i]
        return carry

    lax.fori_loop(0, GROUPS, conv_step, 0, unroll=UNROLL)
    for r in range(ROWS):
        wet = wet_ref[0:1, lanes(r)]
        og = cot_ref[:, lanes(r)].astype(f32) * wet
        igrad_ref[:, lanes(r)] = (wet * (og + conv_ref[:, lanes(r)])).astype(bf16)


def unpack_kernel(factor, core_ref, mine_ref, other_ref, gin_ref, gout_ref, gkern_ref, *rest):
    *vec_refs, gbias_ref, full_ref = rest
    core = core_ref[0]
    full_ref[core] = mine_ref[...].astype(f32) * factor
    full_ref[1 - core] = other_ref[...].astype(f32) * factor
    for blk in range(BLOCKS):
        begin, end = blk * COLS, min((blk + 1) * COLS, HID)
        gin_ref[:, begin:end] = full_ref[0, blk * CX : blk * CX + C, 0 : end - begin]
        gbias_ref[begin:end] = full_ref[0, blk * CX + C, 0 : end - begin]
        gout_ref[:, begin:end] = full_ref[1, blk * CX : blk * CX + C, 0 : end - begin]
    for half, begin, end in ((0, 0, COLS), (1, COLS, C)):
        small = full_ref[half, SMALL : SMALL + 2 * PAIRS + 2, 0 : end - begin]
        gkern_ref[:, begin:end] = small[0:TAPS]
        for s, ref in enumerate(vec_refs):
            ref[:, begin:end] = small[TAPS + s : TAPS + s + 1]


def near(x):
    return pltpu.with_memory_space_constraint(x, pltpu.VMEM)


def hbm(shape, dtype):
    return jax.ShapeDtypeStruct(shape, dtype)


def call(kernel, outs, n_smem, args, scratch=(), time=1.0, limit=8, n_far=None):
    n_far = n_smem if n_far is None else n_far
    far = [pltpu.with_memory_space_constraint(x, pltpu.HBM) for x in args[:n_far]]
    args = far + [near(x) for x in args[n_far:]]
    return pl.pallas_call(
        kernel,
        out_shape=outs,
        in_specs=[SMEM] * n_smem + [VMEM] * (len(args) - n_smem),
        out_specs=[VMEM] * len(outs),
        scratch_shapes=[pltpu.VMEM(s, d) for s, d in scratch],
        cost_estimate=pl.CostEstimate(flops=int(time * 1.1e9), bytes_accessed=1000000, transcendentals=0),
        compiler_params=pltpu.CompilerParams(vmem_limit_bytes=limit * MIB),
    )(*args)


TILE_AXES = ("y", "z", "core")
PLANE = ("y", "rep")


def shifted(value, steps):
    count = lax.axis_size(TILE_AXES)
    first, last = max(0, -steps), min(count, count - steps)
    return lax.ppermute(value, TILE_AXES, [(s, s + steps) for s in range(first, last)])


def exchange(value, axes):
    return lax.all_to_all(value, axes, 0, 0, tiled=True)


def add_kernel(keep_ref, got_ref, pair_ref):
    pair_ref[...] = (keep_ref[...].astype(f32) + got_ref[...].astype(f32)).astype(bf16)


def fold_kernel(value_ref, copies_ref):
    total = value_ref[0].astype(f32)
    for k in range(1, value_ref.shape[0]):
        total = total + value_ref[k].astype(f32)
    total = total.astype(bf16)
    for k in range(copies_ref.shape[0]):
        copies_ref[k] = total


def fold(value, axes, next_axes):
    count, copies = lax.axis_size(axes), lax.axis_size(next_axes)
    rows = value.shape[0] // count
    (out,) = call(
        fold_kernel,
        [pltpu.VMEM((copies, rows, COLS), bf16)],
        0,
        [value.reshape(count, rows, COLS)],
        limit=4,
    )
    return out.reshape(copies * rows, COLS)


def reduce_pack(keep, send):
    swap = [(0, 1), (1, 0)]
    got = lax.ppermute(send, "core", swap)
    (pair,) = call(add_kernel, [pltpu.VMEM((HALF, COLS), bf16)], 0, [keep, got], limit=4)
    part = exchange(pair, PLANE)
    part = fold(part, PLANE, "z")
    part = exchange(part, "z")
    part = fold(part, "z", PLANE)
    mine = exchange(part, PLANE)
    return mine, lax.ppermute(mine, "core", swap)


def step(
    fields,
    wet_bits,
    neighbours,
    kernel,
    conv_bias,
    ln_gain,
    ln_shift,
    in_weight,
    in_bias,
    out_weight,
    out_bias,
    cotangent,
):
    act2 = (C, CELLS)
    slot = lax.axis_index(TILE_AXES).astype(jnp.int32).reshape(1)
    core = lax.axis_index("core").astype(jnp.int32).reshape(1)
    cot = cotangent.reshape(act2)
    masked, wet = call(
        mask_kernel,
        [pltpu.VMEM(act2, bf16), pltpu.VMEM((8, CELLS), f32)],
        1,
        [wet_bits.transpose(2, 0, 1), fields.reshape(act2)],
        limit=4,
        n_far=2,
    )
    from_north = shifted(masked, 1)
    from_south = shifted(masked, -1)
    vectors = [v[None, :] for v in (conv_bias, ln_gain, ln_shift, out_bias)]
    high = lax.reduce_precision(in_bias, 8, 7)
    bias_rows = jnp.stack([high, in_bias - high]).astype(bf16)
    inwt = jnp.concatenate([in_weight, bias_rows, jnp.zeros((CX - C - 2, HID), bf16)], axis=0).T
    cot, inwt = lax.optimization_barrier((cot, inwt))
    table, masks, coef, chans, part, ograd, agrad, osum = call(
        pre_kernel,
        [
            pltpu.VMEM((C, COLS), f32),
            pltpu.VMEM((21, 8, COLS), f32),
            pltpu.VMEM((TAPS, C, COLS), f32),
            pltpu.VMEM((4, C, COLS), f32),
            pltpu.VMEM(act2, f32),
            pltpu.VMEM((CX, CELLS), bf16),
            pltpu.VMEM((HID, CELLS), f32),
            pltpu.VMEM((C, COLS), f32),
        ],
        2,
        [slot, neighbours, masked, wet, cot, kernel.T] + vectors + [out_weight],
        [((ROWS, C, COLS), f32), ((COLS, 2 * COLS), f32)],
        time=6.0,
        limit=8,
    )
    cgrad, act, keep, send = call(
        main_kernel,
        [
            pltpu.VMEM(act2, bf16),
            pltpu.VMEM((HID, CELLS), bf16),
            pltpu.VMEM((HALF, COLS), bf16),
            pltpu.VMEM((HALF, COLS), bf16),
        ],
        1,
        [
            core,
            masked,
            from_north,
            from_south,
            masks,
            coef,
            chans,
            part,
            ograd,
            agrad,
            osum,
            in_weight,
            inwt,
        ],
        [
            ((4 * ROWS, C, COLS), f32),
            (act2, f32),
            ((8, CELLS), f32),
            ((HID, CELLS), f32),
            ((CX, CELLS), bf16),
            ((HID, CELLS), bf16),
            ((PAIRS, C, 2 * COLS), bf16),
            ((2 * PAIRS + 2, 2 * COLS), f32),
            ((2, HALF, COLS), bf16),
        ],
        time=12.0,
        limit=24,
    )
    cg_north = shifted(cgrad, 1)
    cg_south = shifted(cgrad, -1)
    (field,) = call(
        field_kernel,
        [hbm(act2, bf16)],
        0,
        [masked, wet, table, act, out_weight.T],
        [(act2, f32)],
        time=1.5,
        limit=4,
    )
    (input_grad,) = call(
        back_kernel,
        [hbm(act2, bf16)],
        2,
        [slot, neighbours, cgrad, cg_north, cg_south, wet, cot, table],
        [((21, 8, COLS), f32), ((3 * ROWS, C, COLS), f32), (act2, f32), ((TAPS, C, COLS), f32)],
        time=6.0,
        limit=14,
    )
    mine, other = reduce_pack(keep, send)
    total_cells = lax.axis_size(TILE_AXES) * lax.axis_size("rep") * CELLS
    factor = float(total_cells) ** -0.5
    gin, gout, gkern, gbias, ggain, gshift, gobias, gibias = call(
        lambda *refs: unpack_kernel(factor, *refs),
        [hbm((C, HID), f32), hbm((C, HID), f32), hbm((TAPS, C), f32)] + [hbm((1, C), f32)] * 4 + [hbm((HID,), f32)],
        1,
        [core, mine, other],
        [((2, HALF, COLS), f32)],
        limit=8,
    )
    return (
        field.reshape(1, 1, C, CELLS),
        input_grad.reshape(1, 1, C, CELLS),
        gkern.T,
        gbias.reshape(C),
        ggain.reshape(C),
        gshift.reshape(C),
        gin,
        gibias,
        gout.T,
        gobias.reshape(C),
    )


def solution(mesh):
    rep = mesh.shape["rep"]
    fine = Mesh(mesh.devices.reshape(4, -1, 2, rep), ("y", "z", "core", "rep"))
    tile = P("rep", TILE_AXES, None, None)
    placed = (tile, P(TILE_AXES, None, None), P(TILE_AXES, None)) + (P(),) * 8 + (tile,)
    return jax.shard_map(
        step,
        mesh=fine,
        in_specs=placed,
        out_specs=(tile, tile) + (P(),) * 8,
        check_vma=False,
    )
```

```python
import jax
import jax.numpy as jnp
from jax import lax
from jax.experimental import pallas as pl
from jax.experimental.pallas import tpu as pltpu
from jax.sharding import Mesh, PartitionSpec as P


C = 200
CX = 208
HID = 800
ROWS = 6
COLS = 128
CELLS = 768
WORDS = 5
BITS = 30
TAPS = 49
GROUPS = C // 8
BLOCKS = 7
HALF = 1408
SMALL = HID - 6 * COLS
VECTORS = SMALL + TAPS
PAIRS = 27
MIB = 1 << 20
UNROLL = 5

bf16 = jnp.bfloat16
f32 = jnp.float32
gelu_scale = 0.7978845608028654
VMEM = pl.BlockSpec(memory_space=pltpu.VMEM)
SMEM = pl.BlockSpec(memory_space=pltpu.SMEM)
NT_DIMS = (((1,), (1,)), ((), ()))
NORTH, OWN, SOUTH = 0, 1, 2


def row_class(row):
    return row // ROWS


def lanes(r):
    return slice(r * COLS, (r + 1) * COLS)


def wet_row(bits_ref, r):
    col = lax.broadcasted_iota(jnp.int32, (8, COLS), 1)
    word = jnp.zeros((8, COLS), jnp.int32)
    shift = col
    for w in range(WORDS):
        word = jnp.where(col >= BITS * w, bits_ref[w, 0, r], word)
        shift = jnp.where(col >= BITS * w, col - BITS * w, shift)
    return jnp.bitwise_and(jnp.right_shift(word, shift), 1).astype(f32)


def mask_kernel(bits_ref, fields_ref, masked_ref, wet_ref):
    for r in range(ROWS):
        wet = wet_row(bits_ref, r)
        wet_ref[:, lanes(r)] = wet
        masked_ref[:, lanes(r)] = (fields_ref[:, lanes(r)].astype(f32) * wet[0:1]).astype(bf16)


def fill_masks(slot_ref, near_ref, masks_ref):
    slot = slot_ref[0]

    def flag(k, step):
        return jnp.where(near_ref[0, k] == slot + step, 1.0, 0.0).astype(f32)

    lane = lax.broadcasted_iota(jnp.int32, (8, COLS), 1)
    triples = (
        (flag(0, -1), flag(4, -1), flag(5, -1)),
        (jnp.float32(1.0), flag(2, 0), flag(3, 0)),
        (flag(1, 1), flag(6, 1), flag(7, 1)),
    )
    for cls, (centre, west, east) in enumerate(triples):
        for b in range(7):
            off = 2 * b - 6
            mask = jnp.full((8, COLS), centre, f32)
            if off > 0:
                mask = jnp.where(lane < off, jnp.full((8, COLS), east, f32), mask)
            if off < 0:
                mask = jnp.where(lane >= COLS + off, jnp.full((8, COLS), west, f32), mask)
            masks_ref[7 * cls + b] = mask


def fill_rows(ref, part, rows_ref):
    for r in range(ROWS):
        rows_ref[ROWS * part + r] = ref[:, lanes(r)].astype(f32)


def conv_group(rows, coef, masks_ref, classes):
    total = [None] * ROWS
    for b in range(7):
        off = 2 * b - 6
        masked = {}
        for r in rows:
            plain = b == 3 and row_class(r) == OWN
            masked[r] = rows[r] if plain else rows[r] * masks_ref[7 * row_class(r) + b]
        taps = [coef(a, b) for a in range(7)]
        for i in range(ROWS):
            acc = None
            for a in range(7):
                if row_class(i + 2 * a) in classes:
                    term = taps[a] * masked[i + 2 * a]
                    acc = term if acc is None else acc + term
            if off != 0:
                acc = pltpu.roll(acc, (-off) % COLS, 1)
            total[i] = acc if total[i] is None else total[i] + acc
    return total


def fill_coef(table_ref, coef_ref):
    for t in range(TAPS):
        coef_ref[t] = jnp.broadcast_to(table_ref[:, t : t + 1], (C, COLS))


def pre_kernel(
    slot_ref,
    near_ref,
    own_ref,
    wet_ref,
    cot_ref,
    kern_ref,
    vec0_ref,
    vec1_ref,
    vec2_ref,
    vec3_ref,
    outw_ref,
    table_ref,
    masks_ref,
    coef_ref,
    chans_ref,
    part_ref,
    ograd_ref,
    agrad_ref,
    osum_ref,
    rows_ref,
    flat_ref,
):
    flat_ref[...] = jnp.zeros(flat_ref.shape, f32)
    flat_ref[0:TAPS, 0:C] = kern_ref[...]
    for k, vec_ref in enumerate((vec0_ref, vec1_ref, vec2_ref, vec3_ref)):
        flat_ref[TAPS + k : TAPS + k + 1, 0:C] = vec_ref[...]
    table_ref[0:COLS, :] = flat_ref[:, 0:COLS].T
    table_ref[COLS:C, :] = flat_ref[:, COLS:].T[0 : C - COLS, :]
    fill_masks(slot_ref, near_ref, masks_ref)
    fill_rows(own_ref, 0, rows_ref)
    osum = jnp.zeros((C, COLS), f32)
    for r in range(ROWS):
        og = cot_ref[:, lanes(r)].astype(f32) * wet_ref[0:1, lanes(r)]
        osum = osum + og
        ograd_ref[:, lanes(r)] = jnp.concatenate([og, jnp.zeros((CX - C, COLS), f32)], axis=0).astype(bf16)
    osum_ref[...] = osum
    agrad_ref[...] = jnp.dot(outw_ref[...], ograd_ref[0:C, :], preferred_element_type=f32)
    fill_coef(table_ref, coef_ref)
    for k in range(4):
        chans_ref[k] = jnp.broadcast_to(table_ref[:, TAPS + k : TAPS + k + 1], (C, COLS))

    def step(g, carry):
        at = pl.ds(pl.multiple_of(g * 8, 8), 8)
        rows = {ROWS + r: rows_ref[r, at, :] for r in range(ROWS)}
        total = conv_group(rows, lambda a, b: coef_ref[7 * a + b, at, :], masks_ref, (OWN,))
        for i in range(ROWS):
            part_ref[at, lanes(i)] = total[i] + chans_ref[0, at, :]
        return carry

    lax.fori_loop(0, GROUPS, step, 0, unroll=UNROLL)


def main_kernel(
    core_ref,
    own_ref,
    north_ref,
    south_ref,
    masks_ref,
    coef_ref,
    chans_ref,
    part_ref,
    ograd_ref,
    agrad_ref,
    osum_ref,
    inw_ref,
    inwt_ref,
    cgrad_ref,
    act_ref,
    keep_ref,
    send_ref,
    rows_ref,
    vecs_ref,
    conv_ref,
    istd_ref,
    hid_ref,
    norm_ref,
    hgrad_ref,
    bias_ref,
    pack_ref,
):
    fill_rows(north_ref, NORTH, rows_ref)
    fill_rows(own_ref, OWN, rows_ref)
    fill_rows(south_ref, SOUTH, rows_ref)

    def conv_step(g, carry):
        at = pl.ds(pl.multiple_of(g * 8, 8), 8)
        rows = {r: rows_ref[r, at, :] for r in range(3 * ROWS) if row_class(r) != OWN}
        total = conv_group(rows, lambda a, b: coef_ref[7 * a + b, at, :], masks_ref, (NORTH, SOUTH))
        for i in range(ROWS):
            conv_ref[at, lanes(i)] = total[i] + part_ref[at, lanes(i)]
        return carry

    lax.fori_loop(0, GROUPS, conv_step, 0, unroll=UNROLL)

    extra = lax.broadcasted_iota(jnp.int32, (8, COLS), 0)
    extra = jnp.where(extra < 2, 1.0, 0.0).astype(f32)
    for r in range(ROWS):
        x = conv_ref[:, lanes(r)]
        mean = jnp.sum(x, axis=0, keepdims=True) * (1.0 / C)
        x = x - mean
        var = jnp.sum(x * x, axis=0, keepdims=True) * (1.0 / C)
        istd = lax.rsqrt(var + 1e-06)
        normed = x * istd
        conv_ref[:, lanes(r)] = normed
        istd_ref[:, lanes(r)] = jnp.broadcast_to(istd, (8, COLS))
        no = jnp.concatenate([normed * chans_ref[1] + chans_ref[2], extra], axis=0)
        norm_ref[:, lanes(r)] = no.astype(bf16)

    hid_ref[...] = jnp.dot(inwt_ref[...], norm_ref[...], preferred_element_type=f32)

    def gelu_step(i, carry):
        at = pl.ds(pl.multiple_of(i * 16, 16), 16)
        h = hid_ref[at, :]
        h2 = h * h
        t = jnp.tanh(h * (gelu_scale + (gelu_scale * 0.044715) * h2))
        half = 0.5 + 0.5 * t
        act_ref[at, :] = (h * half).astype(bf16)
        slope = (0.5 * gelu_scale) + (0.5 * gelu_scale * 3.0 * 0.044715) * h2
        deriv = half + h * (1.0 - t * t) * slope
        hgrad_ref[at, :] = (agrad_ref[at, :] * deriv).astype(bf16)
        return carry

    lax.fori_loop(0, HID // 16, gelu_step, 0, unroll=2)

    hid_ref[0:C, :] = jnp.dot(inw_ref[...], hgrad_ref[...], preferred_element_type=f32)
    gsum = jnp.zeros((C, COLS), f32)
    ssum = jnp.zeros((C, COLS), f32)
    bsum = jnp.zeros((C, COLS), f32)
    cg_base = 3 * ROWS
    for r in range(ROWS):
        ng = hid_ref[0:C, lanes(r)]
        normed = conv_ref[:, lanes(r)]
        ssum = ssum + ng
        gsum = gsum + ng * normed
        scaled = ng * chans_ref[1]
        m1 = jnp.sum(scaled, axis=0, keepdims=True) * (1.0 / C)
        m2 = jnp.sum(scaled * normed, axis=0, keepdims=True) * (1.0 / C)
        cg = (istd_ref[0:1, lanes(r)] * (scaled - m1 - normed * m2)).astype(bf16)
        cgrad_ref[:, lanes(r)] = cg
        rows_ref[cg_base + r] = cg.astype(f32)
        bsum = bsum + cg.astype(f32)
    for s, vec in enumerate((bsum, gsum, ssum, osum_ref[...])):
        vecs_ref[s] = vec

    bias_ref[...] = jnp.zeros(bias_ref.shape, f32)

    for half, (left_ref, right_ref) in enumerate(((norm_ref, hgrad_ref), (ograd_ref, act_ref))):
        for first in range(0, HID, 2 * COLS):
            last = min(first + 2 * COLS, HID)
            blk = first // COLS
            part = lax.dot_general(left_ref[...], right_ref[first:last, :], NT_DIMS, preferred_element_type=f32)
            if last - first < COLS:
                part = jnp.concatenate([part, jnp.zeros((CX, COLS - (last - first)), f32)], axis=1)
            for sub in range(max(1, (last - first) // COLS)):
                piece = part[:, lanes(sub)]
                if half == 0:
                    bias_ref[blk + sub : blk + sub + 1, :] = piece[C : C + 1, :]
                piece = piece[0:C, :]
                pack_ref[half, (blk + sub) * C : (blk + sub + 1) * C, :] = piece.astype(bf16)
    pack_ref[0, BLOCKS * C :, :] = bias_ref[...].astype(bf16)
    pack_ref[1, BLOCKS * C :, :] = jnp.zeros((8, COLS), bf16)
    core = core_ref[0]
    keep_ref[...] = pack_ref[core]
    send_ref[...] = pack_ref[1 - core]


def taps_kernel(rows_ref, masks_ref, vecs_ref, out_ref, sums_ref, small_ref):
    cg_base = 3 * ROWS
    for s in range(5):
        vec = vecs_ref[s] if s < 4 else jnp.zeros((C, COLS), f32)
        sums_ref[(TAPS + s) // 2, :, lanes((TAPS + s) % 2)] = vec.astype(bf16)

    def tap_step(g, carry):
        at = pl.ds(pl.multiple_of(g * 8, 8), 8)
        for b in range(7):
            off = 2 * b - 6
            acc = [None] * 7
            for i in range(ROWS):
                turned = rows_ref[cg_base + i, at, :]
                if off != 0:
                    turned = pltpu.roll(turned, off % COLS, 1)
                parts = [turned if b == 3 and cls == OWN else turned * masks_ref[7 * cls + b] for cls in range(3)]
                for a in range(7):
                    r = i + 2 * a
                    term = parts[row_class(r)] * rows_ref[r, at, :]
                    acc[a] = term if acc[a] is None else acc[a] + term
            for a in range(7):
                t = 7 * a + b
                sums_ref[t // 2, at, lanes(t % 2)] = acc[a].astype(bf16)
        return carry

    lax.fori_loop(0, GROUPS, tap_step, 0, unroll=UNROLL)
    lane = lax.broadcasted_iota(jnp.int32, (8, 2 * COLS), 1)
    line = lax.broadcasted_iota(jnp.int32, (8, 2 * COLS), 0)
    pick = jnp.where((lane >= COLS) == (line == 1), jnp.where(line < 2, 1.0, 0.0), 0.0).astype(bf16)
    small_ref[...] = jnp.zeros(small_ref.shape, f32)
    for k in range(PAIRS):
        both = lax.dot_general(pick, sums_ref[k], NT_DIMS, preferred_element_type=f32)
        small_ref[SMALL + 2 * k : SMALL + 2 * k + 2, 0:C] = both[0:2, :]
    out_ref[0:COLS, :] = small_ref[:, 0:COLS].T
    out_ref[COLS:, :] = small_ref[:, COLS:].T[0 : C - COLS, :]


def field_kernel(own_ref, wet_ref, table_ref, act_ref, outwt_ref, field_ref, hid_ref):
    hid_ref[...] = jnp.dot(outwt_ref[...], act_ref[...], preferred_element_type=f32)
    bias = jnp.broadcast_to(table_ref[:, TAPS + 3 : TAPS + 4], (C, COLS))
    for r in range(ROWS):
        update = hid_ref[:, lanes(r)] + bias
        own = own_ref[:, lanes(r)].astype(f32)
        field_ref[:, lanes(r)] = (wet_ref[0:1, lanes(r)] * (own + update)).astype(bf16)


def back_kernel(
    slot_ref,
    near_ref,
    own_ref,
    north_ref,
    south_ref,
    wet_ref,
    cot_ref,
    table_ref,
    igrad_ref,
    masks_ref,
    rows_ref,
    conv_ref,
    coef_ref,
):
    fill_masks(slot_ref, near_ref, masks_ref)
    fill_coef(table_ref, coef_ref)
    fill_rows(north_ref, NORTH, rows_ref)
    fill_rows(own_ref, OWN, rows_ref)
    fill_rows(south_ref, SOUTH, rows_ref)

    def conv_step(g, carry):
        at = pl.ds(pl.multiple_of(g * 8, 8), 8)
        rows = {r: rows_ref[r, at, :] for r in range(3 * ROWS)}
        total = conv_group(
            rows, lambda a, b: coef_ref[TAPS - 1 - 7 * a - b, at, :], masks_ref, (NORTH, OWN, SOUTH)
        )
        for i in range(ROWS):
            conv_ref[at, lanes(i)] = total[i]
        return carry

    lax.fori_loop(0, GROUPS, conv_step, 0, unroll=UNROLL)
    for r in range(ROWS):
        wet = wet_ref[0:1, lanes(r)]
        og = cot_ref[:, lanes(r)].astype(f32) * wet
        igrad_ref[:, lanes(r)] = (wet * (og + conv_ref[:, lanes(r)])).astype(bf16)


def unpack_kernel(factor, core_ref, mine_ref, other_ref, gin_ref, gout_ref, gkern_ref, *rest):
    *vec_refs, gbias_ref, full_ref = rest
    core = core_ref[0]
    full_ref[core] = mine_ref[...].astype(f32) * factor
    full_ref[1 - core] = other_ref[...].astype(f32) * factor
    for blk in range(BLOCKS):
        begin, end = blk * COLS, min((blk + 1) * COLS, HID)
        gin_ref[:, begin:end] = full_ref[0, blk * C : (blk + 1) * C, 0 : end - begin]
        gbias_ref[begin:end] = full_ref[0, BLOCKS * C + blk, 0 : end - begin]
        gout_ref[:, begin:end] = full_ref[1, blk * C : (blk + 1) * C, 0 : end - begin]
    last = slice((BLOCKS - 1) * C, BLOCKS * C)
    columns = (full_ref[0, last, :] + full_ref[1, last, :]).T
    gkern_ref[...] = columns[SMALL:VECTORS, :]
    for s, ref in enumerate(vec_refs):
        ref[...] = columns[VECTORS + s : VECTORS + s + 1, :]


def near(x):
    return pltpu.with_memory_space_constraint(x, pltpu.VMEM)


def hbm(shape, dtype):
    return jax.ShapeDtypeStruct(shape, dtype)


def call(kernel, outs, n_smem, args, scratch=(), time=1.0, limit=8, n_far=None):
    n_far = n_smem if n_far is None else n_far
    far = [pltpu.with_memory_space_constraint(x, pltpu.HBM) for x in args[:n_far]]
    args = far + [near(x) for x in args[n_far:]]
    return pl.pallas_call(
        kernel,
        out_shape=outs,
        in_specs=[SMEM] * n_smem + [VMEM] * (len(args) - n_smem),
        out_specs=[VMEM] * len(outs),
        scratch_shapes=[pltpu.VMEM(s, d) for s, d in scratch],
        cost_estimate=pl.CostEstimate(flops=int(time * 1.1e9), bytes_accessed=1000000, transcendentals=0),
        compiler_params=pltpu.CompilerParams(vmem_limit_bytes=limit * MIB),
    )(*args)


TILE_AXES = ("y", "z", "core")
PLANE = ("y", "rep")


def shifted(value, steps):
    count = lax.axis_size(TILE_AXES)
    first, last = max(0, -steps), min(count, count - steps)
    return lax.ppermute(value, TILE_AXES, [(s, s + steps) for s in range(first, last)])


def exchange(value, axes):
    return lax.all_to_all(value, axes, 0, 0, tiled=True)


def add_kernel(keep_ref, got_ref, small_ref, pair_ref):
    last = (BLOCKS - 1) * C
    total = keep_ref[...].astype(f32) + got_ref[...].astype(f32)
    pair_ref[...] = total.astype(bf16)
    pair_ref[last : last + C, :] = (total[last : last + C, :] + small_ref[...]).astype(bf16)


def fold_kernel(value_ref, copies_ref):
    total = value_ref[0].astype(f32)
    for k in range(1, value_ref.shape[0]):
        total = total + value_ref[k].astype(f32)
    total = total.astype(bf16)
    for k in range(copies_ref.shape[0]):
        copies_ref[k] = total


def fold(value, axes, next_axes):
    count, copies = lax.axis_size(axes), lax.axis_size(next_axes)
    rows = value.shape[0] // count
    (out,) = call(
        fold_kernel,
        [pltpu.VMEM((copies, rows, COLS), bf16)],
        0,
        [value.reshape(count, rows, COLS)],
        limit=4,
    )
    return out.reshape(copies * rows, COLS)


def reduce_pack(keep, send, small):
    swap = [(0, 1), (1, 0)]
    got = lax.ppermute(send, "core", swap)
    (pair,) = call(add_kernel, [pltpu.VMEM((HALF, COLS), bf16)], 0, [keep, got, small], limit=4)
    part = exchange(pair, PLANE)
    part = fold(part, PLANE, "z")
    part = exchange(part, "z")
    part = fold(part, "z", PLANE)
    mine = exchange(part, PLANE)
    return mine, lax.ppermute(mine, "core", swap)


def step(
    fields,
    wet_bits,
    neighbours,
    kernel,
    conv_bias,
    ln_gain,
    ln_shift,
    in_weight,
    in_bias,
    out_weight,
    out_bias,
    cotangent,
):
    act2 = (C, CELLS)
    slot = lax.axis_index(TILE_AXES).astype(jnp.int32).reshape(1)
    core = lax.axis_index("core").astype(jnp.int32).reshape(1)
    cot = cotangent.reshape(act2)
    masked, wet = call(
        mask_kernel,
        [pltpu.VMEM(act2, bf16), pltpu.VMEM((8, CELLS), f32)],
        1,
        [wet_bits.transpose(2, 0, 1), fields.reshape(act2)],
        limit=4,
        n_far=2,
    )
    from_north = shifted(masked, 1)
    from_south = shifted(masked, -1)
    vectors = [v[None, :] for v in (conv_bias, ln_gain, ln_shift, out_bias)]
    high = lax.reduce_precision(in_bias, 8, 7)
    bias_rows = jnp.stack([high, in_bias - high]).astype(bf16)
    inwt = jnp.concatenate([in_weight, bias_rows, jnp.zeros((CX - C - 2, HID), bf16)], axis=0).T
    cot, inwt = lax.optimization_barrier((cot, inwt))
    table, masks, coef, chans, part, ograd, agrad, osum = call(
        pre_kernel,
        [
            pltpu.VMEM((C, COLS), f32),
            pltpu.VMEM((21, 8, COLS), f32),
            pltpu.VMEM((TAPS, C, COLS), f32),
            pltpu.VMEM((4, C, COLS), f32),
            pltpu.VMEM(act2, f32),
            pltpu.VMEM((CX, CELLS), bf16),
            pltpu.VMEM((HID, CELLS), f32),
            pltpu.VMEM((C, COLS), f32),
        ],
        2,
        [slot, neighbours, masked, wet, cot, kernel.T] + vectors + [out_weight],
        [((ROWS, C, COLS), f32), ((COLS, 2 * COLS), f32)],
        time=6.0,
        limit=8,
    )
    cgrad, act, keep, send, rows, vecs = call(
        main_kernel,
        [
            pltpu.VMEM(act2, bf16),
            pltpu.VMEM((HID, CELLS), bf16),
            pltpu.VMEM((HALF, COLS), bf16),
            pltpu.VMEM((HALF, COLS), bf16),
            pltpu.VMEM((4 * ROWS, C, COLS), f32),
            pltpu.VMEM((4, C, COLS), f32),
        ],
        1,
        [
            core,
            masked,
            from_north,
            from_south,
            masks,
            coef,
            chans,
            part,
            ograd,
            agrad,
            osum,
            in_weight,
            inwt,
        ],
        [
            (act2, f32),
            ((8, CELLS), f32),
            ((HID, CELLS), f32),
            ((CX, CELLS), bf16),
            ((HID, CELLS), bf16),
            ((8, COLS), f32),
            ((2, HALF, COLS), bf16),
        ],
        time=12.0,
        limit=20,
    )
    cg_north = shifted(cgrad, 1)
    cg_south = shifted(cgrad, -1)
    (small,) = call(
        taps_kernel,
        [pltpu.VMEM((C, COLS), f32)],
        0,
        [rows, masks, vecs],
        [((PAIRS, C, 2 * COLS), bf16), ((COLS, 2 * COLS), f32)],
        time=3.0,
        limit=12,
    )
    (field,) = call(
        field_kernel,
        [hbm(act2, bf16)],
        0,
        [masked, wet, table, act, out_weight.T],
        [(act2, f32)],
        time=1.5,
        limit=4,
    )
    (input_grad,) = call(
        back_kernel,
        [hbm(act2, bf16)],
        2,
        [slot, neighbours, cgrad, cg_north, cg_south, wet, cot, table],
        [((21, 8, COLS), f32), ((3 * ROWS, C, COLS), f32), (act2, f32), ((TAPS, C, COLS), f32)],
        time=6.0,
        limit=14,
    )
    mine, other = reduce_pack(keep, send, small)
    total_cells = lax.axis_size(TILE_AXES) * lax.axis_size("rep") * CELLS
    factor = float(total_cells) ** -0.5
    gin, gout, gkern, gbias, ggain, gshift, gobias, gibias = call(
        lambda *refs: unpack_kernel(factor, *refs),
        [hbm((C, HID), f32), hbm((C, HID), f32), hbm((TAPS, C), f32)] + [hbm((1, C), f32)] * 4 + [hbm((HID,), f32)],
        1,
        [core, mine, other],
        [((2, HALF, COLS), f32)],
        limit=8,
    )
    return (
        field.reshape(1, 1, C, CELLS),
        input_grad.reshape(1, 1, C, CELLS),
        gkern.T,
        gbias.reshape(C),
        ggain.reshape(C),
        gshift.reshape(C),
        gin,
        gibias,
        gout.T,
        gobias.reshape(C),
    )


def solution(mesh):
    rep = mesh.shape["rep"]
    fine = Mesh(mesh.devices.reshape(4, -1, 2, rep), ("y", "z", "core", "rep"))
    tile = P("rep", TILE_AXES, None, None)
    placed = (tile, P(TILE_AXES, None, None), P(TILE_AXES, None)) + (P(),) * 8 + (tile,)
    return jax.shard_map(
        step,
        mesh=fine,
        in_specs=placed,
        out_specs=(tile, tile) + (P(),) * 8,
        check_vma=False,
    )
```

```python
import jax
import jax.numpy as jnp
from jax import lax
from jax.experimental import pallas as pl
from jax.experimental.pallas import tpu as pltpu
from jax.sharding import Mesh, PartitionSpec as P


C = 200
CX = 208
HID = 800
ROWS = 6
COLS = 128
CELLS = 768
WORDS = 5
BITS = 30
TAPS = 49
GROUPS = C // 8
BLOCKS = 7
HALF = 1408
SMALL = HID - 6 * COLS
VECTORS = SMALL + TAPS
PAIRS = 27
MIB = 1 << 20
UNROLL = 5

bf16 = jnp.bfloat16
f32 = jnp.float32
gelu_scale = 0.7978845608028654
VMEM = pl.BlockSpec(memory_space=pltpu.VMEM)
SMEM = pl.BlockSpec(memory_space=pltpu.SMEM)
NT_DIMS = (((1,), (1,)), ((), ()))
NORTH, OWN, SOUTH = 0, 1, 2


def row_class(row):
    return row // ROWS


def lanes(r):
    return slice(r * COLS, (r + 1) * COLS)


def wet_row(bits_ref, r):
    col = lax.broadcasted_iota(jnp.int32, (8, COLS), 1)
    word = jnp.zeros((8, COLS), jnp.int32)
    shift = col
    for w in range(WORDS):
        word = jnp.where(col >= BITS * w, bits_ref[w, 0, r], word)
        shift = jnp.where(col >= BITS * w, col - BITS * w, shift)
    return jnp.bitwise_and(jnp.right_shift(word, shift), 1).astype(f32)


def mask_kernel(bits_ref, fields_ref, masked_ref, wet_ref):
    for r in range(ROWS):
        wet = wet_row(bits_ref, r)
        wet_ref[:, lanes(r)] = wet
        masked_ref[:, lanes(r)] = (fields_ref[:, lanes(r)].astype(f32) * wet[0:1]).astype(bf16)


def fill_masks(slot_ref, near_ref, masks_ref):
    slot = slot_ref[0]

    def flag(k, step):
        return jnp.where(near_ref[0, k] == slot + step, 1.0, 0.0).astype(f32)

    lane = lax.broadcasted_iota(jnp.int32, (8, COLS), 1)
    triples = (
        (flag(0, -1), flag(4, -1), flag(5, -1)),
        (jnp.float32(1.0), flag(2, 0), flag(3, 0)),
        (flag(1, 1), flag(6, 1), flag(7, 1)),
    )
    for cls, (centre, west, east) in enumerate(triples):
        for b in range(7):
            off = 2 * b - 6
            mask = jnp.full((8, COLS), centre, f32)
            if off > 0:
                mask = jnp.where(lane < off, jnp.full((8, COLS), east, f32), mask)
            if off < 0:
                mask = jnp.where(lane >= COLS + off, jnp.full((8, COLS), west, f32), mask)
            masks_ref[7 * cls + b] = mask


def fill_rows(ref, part, rows_ref):
    for r in range(ROWS):
        rows_ref[ROWS * part + r] = ref[:, lanes(r)].astype(f32)


def conv_group(rows, coef, masks_ref, classes):
    total = [None] * ROWS
    for b in range(7):
        off = 2 * b - 6
        masked = {}
        for r in rows:
            plain = b == 3 and row_class(r) == OWN
            masked[r] = rows[r] if plain else rows[r] * masks_ref[7 * row_class(r) + b]
        taps = [coef(a, b) for a in range(7)]
        for i in range(ROWS):
            acc = None
            for a in range(7):
                if row_class(i + 2 * a) in classes:
                    term = taps[a] * masked[i + 2 * a]
                    acc = term if acc is None else acc + term
            if off != 0:
                acc = pltpu.roll(acc, (-off) % COLS, 1)
            total[i] = acc if total[i] is None else total[i] + acc
    return total


def fill_coef(table_ref, store, count):
    table = table_ref[...]
    high = table.astype(bf16)
    low = (table - high.astype(f32)).astype(bf16)
    both = jnp.concatenate([high, low], axis=1)
    ones = jnp.ones((2 * COLS, COLS), bf16)
    lane = lax.broadcasted_iota(jnp.int32, (16, 2 * COLS), 1)
    lane = jnp.bitwise_and(lane, COLS - 1)
    for t in range(count):
        if t % 2 == 0:
            store(t, jnp.broadcast_to(table[:, t : t + 1], (C, COLS)))
            continue
        pick = jnp.where(lane == t, 1.0, 0.0).astype(bf16)
        store(t, jnp.dot(both * pick[0:1, :], ones, preferred_element_type=f32))


def pre_kernel(
    slot_ref,
    near_ref,
    own_ref,
    wet_ref,
    cot_ref,
    kern_ref,
    vec0_ref,
    vec1_ref,
    vec2_ref,
    vec3_ref,
    outw_ref,
    table_ref,
    masks_ref,
    coef_ref,
    chans_ref,
    part_ref,
    ograd_ref,
    agrad_ref,
    osum_ref,
    rows_ref,
    flat_ref,
):
    flat_ref[...] = jnp.zeros(flat_ref.shape, f32)
    flat_ref[0:TAPS, 0:C] = kern_ref[...]
    for k, vec_ref in enumerate((vec0_ref, vec1_ref, vec2_ref, vec3_ref)):
        flat_ref[TAPS + k : TAPS + k + 1, 0:C] = vec_ref[...]
    table_ref[0:COLS, :] = flat_ref[:, 0:COLS].T
    table_ref[COLS:C, :] = flat_ref[:, COLS:].T[0 : C - COLS, :]
    fill_masks(slot_ref, near_ref, masks_ref)
    fill_rows(own_ref, 0, rows_ref)
    osum = jnp.zeros((C, COLS), f32)
    for r in range(ROWS):
        og = cot_ref[:, lanes(r)].astype(f32) * wet_ref[0:1, lanes(r)]
        osum = osum + og
        ograd_ref[:, lanes(r)] = jnp.concatenate([og, jnp.zeros((CX - C, COLS), f32)], axis=0).astype(bf16)
    osum_ref[...] = osum
    agrad_ref[...] = jnp.dot(outw_ref[...], ograd_ref[0:C, :], preferred_element_type=f32)

    def store_pre(t, column):
        if t < TAPS:
            coef_ref[t] = column
        else:
            chans_ref[t - TAPS] = column

    fill_coef(table_ref, store_pre, TAPS + 4)

    def step(g, carry):
        at = pl.ds(pl.multiple_of(g * 8, 8), 8)
        rows = {ROWS + r: rows_ref[r, at, :] for r in range(ROWS)}
        total = conv_group(rows, lambda a, b: coef_ref[7 * a + b, at, :], masks_ref, (OWN,))
        for i in range(ROWS):
            part_ref[at, lanes(i)] = total[i] + chans_ref[0, at, :]
        return carry

    lax.fori_loop(0, GROUPS, step, 0, unroll=UNROLL)


def main_kernel(
    core_ref,
    own_ref,
    north_ref,
    south_ref,
    masks_ref,
    coef_ref,
    chans_ref,
    part_ref,
    ograd_ref,
    agrad_ref,
    osum_ref,
    inw_ref,
    inwt_ref,
    cgrad_ref,
    act_ref,
    keep_ref,
    send_ref,
    rows_ref,
    vecs_ref,
    conv_ref,
    istd_ref,
    hid_ref,
    norm_ref,
    hgrad_ref,
    bias_ref,
    pack_ref,
):
    fill_rows(north_ref, NORTH, rows_ref)
    fill_rows(own_ref, OWN, rows_ref)
    fill_rows(south_ref, SOUTH, rows_ref)

    def conv_step(g, carry):
        at = pl.ds(pl.multiple_of(g * 8, 8), 8)
        rows = {r: rows_ref[r, at, :] for r in range(3 * ROWS) if row_class(r) != OWN}
        total = conv_group(rows, lambda a, b: coef_ref[7 * a + b, at, :], masks_ref, (NORTH, SOUTH))
        for i in range(ROWS):
            conv_ref[at, lanes(i)] = total[i] + part_ref[at, lanes(i)]
        return carry

    lax.fori_loop(0, GROUPS, conv_step, 0, unroll=UNROLL)

    extra = lax.broadcasted_iota(jnp.int32, (8, COLS), 0)
    extra = jnp.where(extra < 2, 1.0, 0.0).astype(f32)
    for r in range(ROWS):
        x = conv_ref[:, lanes(r)]
        mean = jnp.sum(x, axis=0, keepdims=True) * (1.0 / C)
        x = x - mean
        var = jnp.sum(x * x, axis=0, keepdims=True) * (1.0 / C)
        istd = lax.rsqrt(var + 1e-06)
        normed = x * istd
        conv_ref[:, lanes(r)] = normed
        istd_ref[:, lanes(r)] = jnp.broadcast_to(istd, (8, COLS))
        no = jnp.concatenate([normed * chans_ref[1] + chans_ref[2], extra], axis=0)
        norm_ref[:, lanes(r)] = no.astype(bf16)

    hid_ref[...] = jnp.dot(inwt_ref[...], norm_ref[...], preferred_element_type=f32)

    def gelu_step(i, carry):
        at = pl.ds(pl.multiple_of(i * 16, 16), 16)
        h = hid_ref[at, :]
        h2 = h * h
        t = jnp.tanh(h * (gelu_scale + (gelu_scale * 0.044715) * h2))
        half = 0.5 + 0.5 * t
        act_ref[at, :] = (h * half).astype(bf16)
        slope = (0.5 * gelu_scale) + (0.5 * gelu_scale * 3.0 * 0.044715) * h2
        deriv = half + h * (1.0 - t * t) * slope
        hgrad_ref[at, :] = (agrad_ref[at, :] * deriv).astype(bf16)
        return carry

    lax.fori_loop(0, HID // 16, gelu_step, 0, unroll=2)

    hid_ref[0:C, :] = jnp.dot(inw_ref[...], hgrad_ref[...], preferred_element_type=f32)
    gsum = jnp.zeros((C, COLS), f32)
    ssum = jnp.zeros((C, COLS), f32)
    bsum = jnp.zeros((C, COLS), f32)
    cg_base = 3 * ROWS
    for r in range(ROWS):
        ng = hid_ref[0:C, lanes(r)]
        normed = conv_ref[:, lanes(r)]
        ssum = ssum + ng
        gsum = gsum + ng * normed
        scaled = ng * chans_ref[1]
        m1 = jnp.sum(scaled, axis=0, keepdims=True) * (1.0 / C)
        m2 = jnp.sum(scaled * normed, axis=0, keepdims=True) * (1.0 / C)
        cg = (istd_ref[0:1, lanes(r)] * (scaled - m1 - normed * m2)).astype(bf16)
        cgrad_ref[:, lanes(r)] = cg
        rows_ref[cg_base + r] = cg.astype(f32)
        bsum = bsum + cg.astype(f32)
    for s, vec in enumerate((bsum, gsum, ssum, osum_ref[...])):
        vecs_ref[s] = vec

    bias_ref[...] = jnp.zeros(bias_ref.shape, f32)

    for half, (left_ref, right_ref) in enumerate(((norm_ref, hgrad_ref), (ograd_ref, act_ref))):
        for first in range(0, HID, 2 * COLS):
            last = min(first + 2 * COLS, HID)
            blk = first // COLS
            part = lax.dot_general(left_ref[...], right_ref[first:last, :], NT_DIMS, preferred_element_type=f32)
            if last - first < COLS:
                part = jnp.concatenate([part, jnp.zeros((CX, COLS - (last - first)), f32)], axis=1)
            for sub in range(max(1, (last - first) // COLS)):
                piece = part[:, lanes(sub)]
                if half == 0:
                    bias_ref[blk + sub : blk + sub + 1, :] = piece[C : C + 1, :]
                piece = piece[0:C, :]
                pack_ref[half, (blk + sub) * C : (blk + sub + 1) * C, :] = piece.astype(bf16)
    pack_ref[0, BLOCKS * C :, :] = bias_ref[...].astype(bf16)
    pack_ref[1, BLOCKS * C :, :] = jnp.zeros((8, COLS), bf16)
    core = core_ref[0]
    keep_ref[...] = pack_ref[core]
    send_ref[...] = pack_ref[1 - core]


def taps_kernel(rows_ref, masks_ref, vecs_ref, out_ref, sums_ref, small_ref):
    cg_base = 3 * ROWS
    for s in range(5):
        vec = vecs_ref[s] if s < 4 else jnp.zeros((C, COLS), f32)
        sums_ref[(TAPS + s) // 2, :, lanes((TAPS + s) % 2)] = vec.astype(bf16)

    def tap_step(g, carry):
        at = pl.ds(pl.multiple_of(g * 8, 8), 8)
        for b in range(7):
            off = 2 * b - 6
            acc = [None] * 7
            for i in range(ROWS):
                turned = rows_ref[cg_base + i, at, :]
                if off != 0:
                    turned = pltpu.roll(turned, off % COLS, 1)
                parts = [turned if b == 3 and cls == OWN else turned * masks_ref[7 * cls + b] for cls in range(3)]
                for a in range(7):
                    r = i + 2 * a
                    term = parts[row_class(r)] * rows_ref[r, at, :]
                    acc[a] = term if acc[a] is None else acc[a] + term
            for a in range(7):
                t = 7 * a + b
                sums_ref[t // 2, at, lanes(t % 2)] = acc[a].astype(bf16)
        return carry

    lax.fori_loop(0, GROUPS, tap_step, 0, unroll=UNROLL)
    lane = lax.broadcasted_iota(jnp.int32, (8, 2 * COLS), 1)
    line = lax.broadcasted_iota(jnp.int32, (8, 2 * COLS), 0)
    pick = jnp.where((lane >= COLS) == (line == 1), jnp.where(line < 2, 1.0, 0.0), 0.0).astype(bf16)
    small_ref[...] = jnp.zeros(small_ref.shape, f32)
    for k in range(PAIRS):
        both = lax.dot_general(pick, sums_ref[k], NT_DIMS, preferred_element_type=f32)
        small_ref[SMALL + 2 * k : SMALL + 2 * k + 2, 0:C] = both[0:2, :]
    out_ref[0:COLS, :] = small_ref[:, 0:COLS].T
    out_ref[COLS:, :] = small_ref[:, COLS:].T[0 : C - COLS, :]


def field_kernel(own_ref, wet_ref, table_ref, act_ref, outwt_ref, field_ref, hid_ref):
    hid_ref[...] = jnp.dot(outwt_ref[...], act_ref[...], preferred_element_type=f32)
    bias = jnp.broadcast_to(table_ref[:, TAPS + 3 : TAPS + 4], (C, COLS))
    for r in range(ROWS):
        update = hid_ref[:, lanes(r)] + bias
        own = own_ref[:, lanes(r)].astype(f32)
        field_ref[:, lanes(r)] = (wet_ref[0:1, lanes(r)] * (own + update)).astype(bf16)


def back_kernel(
    slot_ref,
    near_ref,
    own_ref,
    north_ref,
    south_ref,
    wet_ref,
    cot_ref,
    table_ref,
    igrad_ref,
    masks_ref,
    rows_ref,
    conv_ref,
    coef_ref,
):
    fill_masks(slot_ref, near_ref, masks_ref)

    def store_back(t, column):
        coef_ref[t] = column

    fill_coef(table_ref, store_back, TAPS)
    fill_rows(north_ref, NORTH, rows_ref)
    fill_rows(own_ref, OWN, rows_ref)
    fill_rows(south_ref, SOUTH, rows_ref)

    def conv_step(g, carry):
        at = pl.ds(pl.multiple_of(g * 8, 8), 8)
        rows = {r: rows_ref[r, at, :] for r in range(3 * ROWS)}
        total = conv_group(
            rows, lambda a, b: coef_ref[TAPS - 1 - 7 * a - b, at, :], masks_ref, (NORTH, OWN, SOUTH)
        )
        for i in range(ROWS):
            conv_ref[at, lanes(i)] = total[i]
        return carry

    lax.fori_loop(0, GROUPS, conv_step, 0, unroll=UNROLL)
    for r in range(ROWS):
        wet = wet_ref[0:1, lanes(r)]
        og = cot_ref[:, lanes(r)].astype(f32) * wet
        igrad_ref[:, lanes(r)] = (wet * (og + conv_ref[:, lanes(r)])).astype(bf16)


def unpack_kernel(factor, core_ref, mine_ref, other_ref, gin_ref, gout_ref, gkern_ref, *rest):
    *vec_refs, gbias_ref, full_ref = rest
    core = core_ref[0]
    full_ref[core] = mine_ref[...].astype(f32) * factor
    full_ref[1 - core] = other_ref[...].astype(f32) * factor
    for blk in range(BLOCKS):
        begin, end = blk * COLS, min((blk + 1) * COLS, HID)
        gin_ref[:, begin:end] = full_ref[0, blk * C : (blk + 1) * C, 0 : end - begin]
        gbias_ref[begin:end] = full_ref[0, BLOCKS * C + blk, 0 : end - begin]
        gout_ref[:, begin:end] = full_ref[1, blk * C : (blk + 1) * C, 0 : end - begin]
    last = slice((BLOCKS - 1) * C, BLOCKS * C)
    columns = (full_ref[0, last, :] + full_ref[1, last, :]).T
    gkern_ref[...] = columns[SMALL:VECTORS, :]
    for s, ref in enumerate(vec_refs):
        ref[...] = columns[VECTORS + s : VECTORS + s + 1, :]


def near(x):
    return pltpu.with_memory_space_constraint(x, pltpu.VMEM)


def hbm(shape, dtype):
    return jax.ShapeDtypeStruct(shape, dtype)


def call(kernel, outs, n_smem, args, scratch=(), time=1.0, limit=8, n_far=None):
    n_far = n_smem if n_far is None else n_far
    far = [pltpu.with_memory_space_constraint(x, pltpu.HBM) for x in args[:n_far]]
    args = far + [near(x) for x in args[n_far:]]
    return pl.pallas_call(
        kernel,
        out_shape=outs,
        in_specs=[SMEM] * n_smem + [VMEM] * (len(args) - n_smem),
        out_specs=[VMEM] * len(outs),
        scratch_shapes=[pltpu.VMEM(s, d) for s, d in scratch],
        cost_estimate=pl.CostEstimate(flops=int(time * 1.1e9), bytes_accessed=1000000, transcendentals=0),
        compiler_params=pltpu.CompilerParams(vmem_limit_bytes=limit * MIB),
    )(*args)


TILE_AXES = ("y", "z", "core")
PLANE = ("y", "rep")


def shifted(value, steps):
    count = lax.axis_size(TILE_AXES)
    first, last = max(0, -steps), min(count, count - steps)
    return lax.ppermute(value, TILE_AXES, [(s, s + steps) for s in range(first, last)])


def exchange(value, axes):
    return lax.all_to_all(value, axes, 0, 0, tiled=True)


def add_kernel(keep_ref, got_ref, small_ref, pair_ref):
    last = (BLOCKS - 1) * C
    total = keep_ref[...].astype(f32) + got_ref[...].astype(f32)
    pair_ref[...] = total.astype(bf16)
    pair_ref[last : last + C, :] = (total[last : last + C, :] + small_ref[...]).astype(bf16)


def fold_kernel(value_ref, copies_ref):
    total = value_ref[0].astype(f32)
    for k in range(1, value_ref.shape[0]):
        total = total + value_ref[k].astype(f32)
    total = total.astype(bf16)
    for k in range(copies_ref.shape[0]):
        copies_ref[k] = total


def fold(value, axes, next_axes):
    count, copies = lax.axis_size(axes), lax.axis_size(next_axes)
    rows = value.shape[0] // count
    (out,) = call(
        fold_kernel,
        [pltpu.VMEM((copies, rows, COLS), bf16)],
        0,
        [value.reshape(count, rows, COLS)],
        limit=4,
    )
    return out.reshape(copies * rows, COLS)


def reduce_pack(keep, send, small):
    swap = [(0, 1), (1, 0)]
    got = lax.ppermute(send, "core", swap)
    (pair,) = call(add_kernel, [pltpu.VMEM((HALF, COLS), bf16)], 0, [keep, got, small], limit=4)
    part = exchange(pair, PLANE)
    part = fold(part, PLANE, "z")
    part = exchange(part, "z")
    part = fold(part, "z", PLANE)
    mine = exchange(part, PLANE)
    return mine, lax.ppermute(mine, "core", swap)


def step(
    fields,
    wet_bits,
    neighbours,
    kernel,
    conv_bias,
    ln_gain,
    ln_shift,
    in_weight,
    in_bias,
    out_weight,
    out_bias,
    cotangent,
):
    act2 = (C, CELLS)
    slot = lax.axis_index(TILE_AXES).astype(jnp.int32).reshape(1)
    core = lax.axis_index("core").astype(jnp.int32).reshape(1)
    cot = cotangent.reshape(act2)
    masked, wet = call(
        mask_kernel,
        [pltpu.VMEM(act2, bf16), pltpu.VMEM((8, CELLS), f32)],
        1,
        [wet_bits.transpose(2, 0, 1), fields.reshape(act2)],
        limit=4,
        n_far=2,
    )
    from_north = shifted(masked, 1)
    from_south = shifted(masked, -1)
    vectors = [v[None, :] for v in (conv_bias, ln_gain, ln_shift, out_bias)]
    high = lax.reduce_precision(in_bias, 8, 7)
    bias_rows = jnp.stack([high, in_bias - high]).astype(bf16)
    inwt = jnp.concatenate([in_weight, bias_rows, jnp.zeros((CX - C - 2, HID), bf16)], axis=0).T
    cot, inwt = lax.optimization_barrier((cot, inwt))
    table, masks, coef, chans, part, ograd, agrad, osum = call(
        pre_kernel,
        [
            pltpu.VMEM((C, COLS), f32),
            pltpu.VMEM((21, 8, COLS), f32),
            pltpu.VMEM((TAPS, C, COLS), f32),
            pltpu.VMEM((4, C, COLS), f32),
            pltpu.VMEM(act2, f32),
            pltpu.VMEM((CX, CELLS), bf16),
            pltpu.VMEM((HID, CELLS), f32),
            pltpu.VMEM((C, COLS), f32),
        ],
        2,
        [slot, neighbours, masked, wet, cot, kernel.T] + vectors + [out_weight],
        [((ROWS, C, COLS), f32), ((COLS, 2 * COLS), f32)],
        time=6.0,
        limit=8,
    )
    cgrad, act, keep, send, rows, vecs = call(
        main_kernel,
        [
            pltpu.VMEM(act2, bf16),
            pltpu.VMEM((HID, CELLS), bf16),
            pltpu.VMEM((HALF, COLS), bf16),
            pltpu.VMEM((HALF, COLS), bf16),
            pltpu.VMEM((4 * ROWS, C, COLS), f32),
            pltpu.VMEM((4, C, COLS), f32),
        ],
        1,
        [
            core,
            masked,
            from_north,
            from_south,
            masks,
            coef,
            chans,
            part,
            ograd,
            agrad,
            osum,
            in_weight,
            inwt,
        ],
        [
            (act2, f32),
            ((8, CELLS), f32),
            ((HID, CELLS), f32),
            ((CX, CELLS), bf16),
            ((HID, CELLS), bf16),
            ((8, COLS), f32),
            ((2, HALF, COLS), bf16),
        ],
        time=12.0,
        limit=20,
    )
    cg_north = shifted(cgrad, 1)
    cg_south = shifted(cgrad, -1)
    (small,) = call(
        taps_kernel,
        [pltpu.VMEM((C, COLS), f32)],
        0,
        [rows, masks, vecs],
        [((PAIRS, C, 2 * COLS), bf16), ((COLS, 2 * COLS), f32)],
        time=3.0,
        limit=12,
    )
    (field,) = call(
        field_kernel,
        [hbm(act2, bf16)],
        0,
        [masked, wet, table, act, out_weight.T],
        [(act2, f32)],
        time=1.5,
        limit=4,
    )
    (input_grad,) = call(
        back_kernel,
        [hbm(act2, bf16)],
        2,
        [slot, neighbours, cgrad, cg_north, cg_south, wet, cot, table],
        [((21, 8, COLS), f32), ((3 * ROWS, C, COLS), f32), (act2, f32), ((TAPS, C, COLS), f32)],
        time=6.0,
        limit=14,
    )
    mine, other = reduce_pack(keep, send, small)
    total_cells = lax.axis_size(TILE_AXES) * lax.axis_size("rep") * CELLS
    factor = float(total_cells) ** -0.5
    gin, gout, gkern, gbias, ggain, gshift, gobias, gibias = call(
        lambda *refs: unpack_kernel(factor, *refs),
        [hbm((C, HID), f32), hbm((C, HID), f32), hbm((TAPS, C), f32)] + [hbm((1, C), f32)] * 4 + [hbm((HID,), f32)],
        1,
        [core, mine, other],
        [((2, HALF, COLS), f32)],
        limit=8,
    )
    return (
        field.reshape(1, 1, C, CELLS),
        input_grad.reshape(1, 1, C, CELLS),
        gkern.T,
        gbias.reshape(C),
        ggain.reshape(C),
        gshift.reshape(C),
        gin,
        gibias,
        gout.T,
        gobias.reshape(C),
    )


def solution(mesh):
    rep = mesh.shape["rep"]
    fine = Mesh(mesh.devices.reshape(4, -1, 2, rep), ("y", "z", "core", "rep"))
    tile = P("rep", TILE_AXES, None, None)
    placed = (tile, P(TILE_AXES, None, None), P(TILE_AXES, None)) + (P(),) * 8 + (tile,)
    return jax.shard_map(
        step,
        mesh=fine,
        in_specs=placed,
        out_specs=(tile, tile) + (P(),) * 8,
        check_vma=False,
    )
```

```python
import jax
import jax.numpy as jnp
from jax import lax
from jax.experimental import pallas as pl
from jax.experimental.pallas import tpu as pltpu
from jax.sharding import Mesh, PartitionSpec as P


C = 200
CX = 208
HID = 800
ROWS = 6
COLS = 128
CELLS = 768
WORDS = 5
BITS = 30
TAPS = 49
GROUPS = C // 8
BLOCKS = 7
HALF = 1408
SMALL = HID - 6 * COLS
VECTORS = SMALL + TAPS
PAIRS = 27
MIB = 1 << 20
UNROLL = 5

bf16 = jnp.bfloat16
f32 = jnp.float32
gelu_scale = 0.7978845608028654
VMEM = pl.BlockSpec(memory_space=pltpu.VMEM)
SMEM = pl.BlockSpec(memory_space=pltpu.SMEM)
NT_DIMS = (((1,), (1,)), ((), ()))
NORTH, OWN, SOUTH = 0, 1, 2


def row_class(row):
    return row // ROWS


def lanes(r):
    return slice(r * COLS, (r + 1) * COLS)


def wet_row(bits_ref, r):
    col = lax.broadcasted_iota(jnp.int32, (8, COLS), 1)
    word = jnp.zeros((8, COLS), jnp.int32)
    shift = col
    for w in range(WORDS):
        word = jnp.where(col >= BITS * w, bits_ref[w, 0, r], word)
        shift = jnp.where(col >= BITS * w, col - BITS * w, shift)
    return jnp.bitwise_and(jnp.right_shift(word, shift), 1).astype(f32)


def mask_kernel(bits_ref, fields_ref, masked_ref, wet_ref):
    for r in range(ROWS):
        wet = wet_row(bits_ref, r)
        wet_ref[:, lanes(r)] = wet
        masked_ref[:, lanes(r)] = (fields_ref[:, lanes(r)].astype(f32) * wet[0:1]).astype(bf16)


def fill_masks(slot_ref, near_ref, masks_ref):
    slot = slot_ref[0]

    def flag(k, step):
        return jnp.where(near_ref[0, k] == slot + step, 1.0, 0.0).astype(f32)

    lane = lax.broadcasted_iota(jnp.int32, (8, COLS), 1)
    triples = (
        (flag(0, -1), flag(4, -1), flag(5, -1)),
        (jnp.float32(1.0), flag(2, 0), flag(3, 0)),
        (flag(1, 1), flag(6, 1), flag(7, 1)),
    )
    for cls, (centre, west, east) in enumerate(triples):
        for b in range(7):
            off = 2 * b - 6
            mask = jnp.full((8, COLS), centre, f32)
            if off > 0:
                mask = jnp.where(lane < off, jnp.full((8, COLS), east, f32), mask)
            if off < 0:
                mask = jnp.where(lane >= COLS + off, jnp.full((8, COLS), west, f32), mask)
            masks_ref[7 * cls + b] = mask


def fill_rows(ref, part, rows_ref):
    for r in range(ROWS):
        rows_ref[ROWS * part + r] = ref[:, lanes(r)].astype(f32)


def conv_group(rows, coef, masks_ref, classes):
    total = [None] * ROWS
    for b in range(7):
        off = 2 * b - 6
        masked = {}
        for r in rows:
            plain = b == 3 and row_class(r) == OWN
            masked[r] = rows[r] if plain else rows[r] * masks_ref[7 * row_class(r) + b]
        taps = [coef(a, b) for a in range(7)]
        for i in range(ROWS):
            acc = None
            for a in range(7):
                if row_class(i + 2 * a) in classes:
                    term = taps[a] * masked[i + 2 * a]
                    acc = term if acc is None else acc + term
            if off != 0:
                acc = pltpu.roll(acc, (-off) % COLS, 1)
            total[i] = acc if total[i] is None else total[i] + acc
    return total


def fill_coef(table_ref, store, count):
    table = table_ref[...]
    high = table.astype(bf16)
    low = (table - high.astype(f32)).astype(bf16)
    both = jnp.concatenate([high, low], axis=1)
    ones = jnp.ones((2 * COLS, COLS), bf16)
    lane = lax.broadcasted_iota(jnp.int32, (16, 2 * COLS), 1)
    lane = jnp.bitwise_and(lane, COLS - 1)
    for t in range(count):
        if t % 2 == 0:
            store(t, jnp.broadcast_to(table[:, t : t + 1], (C, COLS)))
            continue
        pick = jnp.where(lane == t, 1.0, 0.0).astype(bf16)
        store(t, jnp.dot(both * pick[0:1, :], ones, preferred_element_type=f32))


def pre_kernel(
    slot_ref,
    near_ref,
    own_ref,
    wet_ref,
    cot_ref,
    kern_ref,
    vec0_ref,
    vec1_ref,
    vec2_ref,
    vec3_ref,
    outw_ref,
    table_ref,
    masks_ref,
    coef_ref,
    chans_ref,
    part_ref,
    ograd_ref,
    agrad_ref,
    osum_ref,
    rows_ref,
    flat_ref,
):
    flat_ref[...] = jnp.zeros(flat_ref.shape, f32)
    flat_ref[0:TAPS, 0:C] = kern_ref[...]
    for k, vec_ref in enumerate((vec0_ref, vec1_ref, vec2_ref, vec3_ref)):
        flat_ref[TAPS + k : TAPS + k + 1, 0:C] = vec_ref[...]
    table_ref[0:COLS, :] = flat_ref[:, 0:COLS].T
    table_ref[COLS:C, :] = flat_ref[:, COLS:].T[0 : C - COLS, :]
    fill_masks(slot_ref, near_ref, masks_ref)
    fill_rows(own_ref, 0, rows_ref)
    osum = jnp.zeros((C, COLS), f32)
    for r in range(ROWS):
        og = cot_ref[:, lanes(r)].astype(f32) * wet_ref[0:1, lanes(r)]
        osum = osum + og
        ograd_ref[:, lanes(r)] = jnp.concatenate([og, jnp.zeros((CX - C, COLS), f32)], axis=0).astype(bf16)
    osum_ref[...] = osum
    agrad_ref[...] = jnp.dot(outw_ref[...], ograd_ref[0:C, :], preferred_element_type=f32)

    def store_pre(t, column):
        if t < TAPS:
            coef_ref[t] = column
        else:
            chans_ref[t - TAPS] = column

    fill_coef(table_ref, store_pre, TAPS + 4)

    def step(g, carry):
        at = pl.ds(pl.multiple_of(g * 8, 8), 8)
        rows = {ROWS + r: rows_ref[r, at, :] for r in range(ROWS)}
        total = conv_group(rows, lambda a, b: coef_ref[7 * a + b, at, :], masks_ref, (OWN,))
        for i in range(ROWS):
            part_ref[at, lanes(i)] = total[i] + chans_ref[0, at, :]
        return carry

    lax.fori_loop(0, GROUPS, step, 0, unroll=UNROLL)


def main_kernel(
    core_ref,
    own_ref,
    north_ref,
    south_ref,
    masks_ref,
    coef_ref,
    chans_ref,
    part_ref,
    ograd_ref,
    agrad_ref,
    osum_ref,
    inw_ref,
    inwt_ref,
    cgrad_ref,
    act_ref,
    keep_ref,
    send_ref,
    rows_ref,
    vecs_ref,
    conv_ref,
    istd_ref,
    hid_ref,
    norm_ref,
    hgrad_ref,
    bias_ref,
    pack_ref,
):
    fill_rows(north_ref, NORTH, rows_ref)
    fill_rows(own_ref, OWN, rows_ref)
    fill_rows(south_ref, SOUTH, rows_ref)

    def conv_step(g, carry):
        at = pl.ds(pl.multiple_of(g * 8, 8), 8)
        rows = {r: rows_ref[r, at, :] for r in range(3 * ROWS) if row_class(r) != OWN}
        total = conv_group(rows, lambda a, b: coef_ref[7 * a + b, at, :], masks_ref, (NORTH, SOUTH))
        for i in range(ROWS):
            conv_ref[at, lanes(i)] = total[i] + part_ref[at, lanes(i)]
        return carry

    lax.fori_loop(0, GROUPS, conv_step, 0, unroll=UNROLL)

    extra = lax.broadcasted_iota(jnp.int32, (8, COLS), 0)
    extra = jnp.where(extra < 2, 1.0, 0.0).astype(f32)
    for r in range(ROWS):
        x = conv_ref[:, lanes(r)]
        mean = jnp.sum(x, axis=0, keepdims=True) * (1.0 / C)
        x = x - mean
        var = jnp.sum(x * x, axis=0, keepdims=True) * (1.0 / C)
        istd = lax.rsqrt(var + 1e-06)
        normed = x * istd
        conv_ref[:, lanes(r)] = normed
        istd_ref[:, lanes(r)] = jnp.broadcast_to(istd, (8, COLS))
        no = jnp.concatenate([normed * chans_ref[1] + chans_ref[2], extra], axis=0)
        norm_ref[:, lanes(r)] = no.astype(bf16)

    hid_ref[...] = jnp.dot(inwt_ref[...], norm_ref[...], preferred_element_type=f32)

    def gelu_step(i, carry):
        at = pl.ds(pl.multiple_of(i * 16, 16), 16)
        h = hid_ref[at, :]
        h2 = h * h
        t = jnp.tanh(h * (gelu_scale + (gelu_scale * 0.044715) * h2))
        half = 0.5 + 0.5 * t
        act_ref[at, :] = (h * half).astype(bf16)
        slope = (0.5 * gelu_scale) + (0.5 * gelu_scale * 3.0 * 0.044715) * h2
        deriv = half + h * (1.0 - t * t) * slope
        hgrad_ref[at, :] = (agrad_ref[at, :] * deriv).astype(bf16)
        return carry

    lax.fori_loop(0, HID // 16, gelu_step, 0, unroll=2)

    hid_ref[0:C, :] = jnp.dot(inw_ref[...], hgrad_ref[...], preferred_element_type=f32)
    gsum = jnp.zeros((C, COLS), f32)
    ssum = jnp.zeros((C, COLS), f32)
    bsum = jnp.zeros((C, COLS), f32)
    cg_base = 3 * ROWS
    for r in range(ROWS):
        ng = hid_ref[0:C, lanes(r)]
        normed = conv_ref[:, lanes(r)]
        ssum = ssum + ng
        gsum = gsum + ng * normed
        scaled = ng * chans_ref[1]
        m1 = jnp.sum(scaled, axis=0, keepdims=True) * (1.0 / C)
        m2 = jnp.sum(scaled * normed, axis=0, keepdims=True) * (1.0 / C)
        cg = (istd_ref[0:1, lanes(r)] * (scaled - m1 - normed * m2)).astype(bf16)
        cgrad_ref[:, lanes(r)] = cg
        rows_ref[cg_base + r] = cg.astype(f32)
        bsum = bsum + cg.astype(f32)
    for s, vec in enumerate((bsum, gsum, ssum, osum_ref[...])):
        vecs_ref[s] = vec

    bias_ref[...] = jnp.zeros(bias_ref.shape, f32)

    for half, (left_ref, right_ref) in enumerate(((norm_ref, hgrad_ref), (ograd_ref, act_ref))):
        for first in range(0, HID, 2 * COLS):
            last = min(first + 2 * COLS, HID)
            blk = first // COLS
            part = lax.dot_general(left_ref[...], right_ref[first:last, :], NT_DIMS, preferred_element_type=f32)
            if last - first < COLS:
                part = jnp.concatenate([part, jnp.zeros((CX, COLS - (last - first)), f32)], axis=1)
            for sub in range(max(1, (last - first) // COLS)):
                piece = part[:, lanes(sub)]
                if half == 0:
                    bias_ref[blk + sub : blk + sub + 1, :] = piece[C : C + 1, :]
                piece = piece[0:C, :]
                pack_ref[half, (blk + sub) * C : (blk + sub + 1) * C, :] = piece.astype(bf16)
    pack_ref[0, BLOCKS * C :, :] = bias_ref[...].astype(bf16)
    pack_ref[1, BLOCKS * C :, :] = jnp.zeros((8, COLS), bf16)
    core = core_ref[0]
    keep_ref[...] = pack_ref[core]
    send_ref[...] = pack_ref[1 - core]


def taps_kernel(rows_ref, masks_ref, vecs_ref, out_ref, sums_ref, small_ref):
    cg_base = 3 * ROWS
    for s in range(5):
        vec = vecs_ref[s] if s < 4 else jnp.zeros((C, COLS), f32)
        sums_ref[(TAPS + s) // 2, :, lanes((TAPS + s) % 2)] = vec.astype(bf16)

    def tap_step(g, carry):
        at = pl.ds(pl.multiple_of(g * 8, 8), 8)
        for b in range(7):
            off = 2 * b - 6
            acc = [None] * 7
            for i in range(ROWS):
                turned = rows_ref[cg_base + i, at, :]
                if off != 0:
                    turned = pltpu.roll(turned, off % COLS, 1)
                parts = [turned if b == 3 and cls == OWN else turned * masks_ref[7 * cls + b] for cls in range(3)]
                for a in range(7):
                    r = i + 2 * a
                    term = parts[row_class(r)] * rows_ref[r, at, :]
                    acc[a] = term if acc[a] is None else acc[a] + term
            for a in range(7):
                t = 7 * a + b
                sums_ref[t // 2, at, lanes(t % 2)] = acc[a].astype(bf16)
        return carry

    lax.fori_loop(0, GROUPS, tap_step, 0, unroll=UNROLL)
    lane = lax.broadcasted_iota(jnp.int32, (8, 2 * COLS), 1)
    line = lax.broadcasted_iota(jnp.int32, (8, 2 * COLS), 0)
    pick = jnp.where((lane >= COLS) == (line == 1), jnp.where(line < 2, 1.0, 0.0), 0.0).astype(bf16)
    small_ref[...] = jnp.zeros(small_ref.shape, f32)
    for k in range(PAIRS):
        both = lax.dot_general(pick, sums_ref[k], NT_DIMS, preferred_element_type=f32)
        small_ref[SMALL + 2 * k : SMALL + 2 * k + 2, 0:C] = both[0:2, :]
    out_ref[0:COLS, :] = small_ref[:, 0:COLS].T
    out_ref[COLS:, :] = small_ref[:, COLS:].T[0 : C - COLS, :]


def field_kernel(own_ref, wet_ref, table_ref, act_ref, outwt_ref, field_ref, hid_ref):
    hid_ref[...] = jnp.dot(outwt_ref[...], act_ref[...], preferred_element_type=f32)
    bias = jnp.broadcast_to(table_ref[:, TAPS + 3 : TAPS + 4], (C, COLS))
    for r in range(ROWS):
        update = hid_ref[:, lanes(r)] + bias
        own = own_ref[:, lanes(r)].astype(f32)
        field_ref[:, lanes(r)] = (wet_ref[0:1, lanes(r)] * (own + update)).astype(bf16)


def back_kernel(
    slot_ref,
    near_ref,
    own_ref,
    north_ref,
    south_ref,
    wet_ref,
    cot_ref,
    table_ref,
    igrad_ref,
    masks_ref,
    rows_ref,
    conv_ref,
    coef_ref,
):
    fill_masks(slot_ref, near_ref, masks_ref)

    def store_back(t, column):
        coef_ref[t] = column

    fill_coef(table_ref, store_back, TAPS)
    fill_rows(north_ref, NORTH, rows_ref)
    fill_rows(own_ref, OWN, rows_ref)
    fill_rows(south_ref, SOUTH, rows_ref)

    def conv_step(g, carry):
        at = pl.ds(pl.multiple_of(g * 8, 8), 8)
        rows = {r: rows_ref[r, at, :] for r in range(3 * ROWS)}
        total = conv_group(
            rows, lambda a, b: coef_ref[TAPS - 1 - 7 * a - b, at, :], masks_ref, (NORTH, OWN, SOUTH)
        )
        for i in range(ROWS):
            conv_ref[at, lanes(i)] = total[i]
        return carry

    lax.fori_loop(0, GROUPS, conv_step, 0, unroll=UNROLL)
    for r in range(ROWS):
        wet = wet_ref[0:1, lanes(r)]
        og = cot_ref[:, lanes(r)].astype(f32) * wet
        igrad_ref[:, lanes(r)] = (wet * (og + conv_ref[:, lanes(r)])).astype(bf16)


def unpack_kernel(factor, core_ref, mine_ref, other_ref, gin_ref, gout_ref, gkern_ref, *rest):
    *vec_refs, gbias_ref, full_ref = rest
    core = core_ref[0]
    full_ref[core] = mine_ref[...].astype(f32) * factor
    full_ref[1 - core] = other_ref[...].astype(f32) * factor
    for blk in range(BLOCKS):
        begin, end = blk * COLS, min((blk + 1) * COLS, HID)
        gin_ref[:, begin:end] = full_ref[0, blk * C : (blk + 1) * C, 0 : end - begin]
        gbias_ref[begin:end] = full_ref[0, BLOCKS * C + blk, 0 : end - begin]
        gout_ref[:, begin:end] = full_ref[1, blk * C : (blk + 1) * C, 0 : end - begin]
    last = slice((BLOCKS - 1) * C, BLOCKS * C)
    columns = (full_ref[0, last, :] + full_ref[1, last, :]).T
    gkern_ref[...] = columns[SMALL:VECTORS, :]
    for s, ref in enumerate(vec_refs):
        ref[...] = columns[VECTORS + s : VECTORS + s + 1, :]


def near(x):
    return pltpu.with_memory_space_constraint(x, pltpu.VMEM)


def hbm(shape, dtype):
    return jax.ShapeDtypeStruct(shape, dtype)


def call(kernel, outs, n_smem, args, scratch=(), time=1.0, limit=8, n_far=None):
    n_far = n_smem if n_far is None else n_far
    far = [pltpu.with_memory_space_constraint(x, pltpu.HBM) for x in args[:n_far]]
    args = far + [near(x) for x in args[n_far:]]
    return pl.pallas_call(
        kernel,
        out_shape=outs,
        in_specs=[SMEM] * n_smem + [VMEM] * (len(args) - n_smem),
        out_specs=[VMEM] * len(outs),
        scratch_shapes=[pltpu.VMEM(s, d) for s, d in scratch],
        cost_estimate=pl.CostEstimate(flops=int(time * 1.1e9), bytes_accessed=1000000, transcendentals=0),
        compiler_params=pltpu.CompilerParams(vmem_limit_bytes=limit * MIB),
    )(*args)


TILE_AXES = ("y", "z", "core")
PLANE = ("y", "rep")


def shifted(value, steps):
    count = lax.axis_size(TILE_AXES)
    first, last = max(0, -steps), min(count, count - steps)
    return lax.ppermute(value, TILE_AXES, [(s, s + steps) for s in range(first, last)])


def exchange(value, axes):
    return lax.all_to_all(value, axes, 0, 0, tiled=True)


def fold_kernel(value_ref, copies_ref):
    total = value_ref[0].astype(f32)
    for k in range(1, value_ref.shape[0]):
        total = total + value_ref[k].astype(f32)
    total = total.astype(bf16)
    for k in range(copies_ref.shape[0]):
        copies_ref[k] = total


def fold(value, axes, next_axes):
    count, copies = lax.axis_size(axes), lax.axis_size(next_axes)
    rows = value.shape[0] // count
    (out,) = call(
        fold_kernel,
        [pltpu.VMEM((copies, rows, COLS), bf16)],
        0,
        [value.reshape(count, rows, COLS)],
        limit=4,
    )
    return out.reshape(copies * rows, COLS)


def reduce_pack(keep, send, small):
    swap = [(0, 1), (1, 0)]
    got = lax.ppermute(send, "core", swap)
    first = (BLOCKS - 1) * C
    small = jnp.pad(small, ((first, HALF - first - C), (0, 0)))
    pair = (keep.astype(f32) + got.astype(f32) + small).astype(bf16)
    part = exchange(pair, PLANE)
    part = fold(part, PLANE, "z")
    part = exchange(part, "z")
    part = fold(part, "z", PLANE)
    mine = exchange(part, PLANE)
    return mine, lax.ppermute(mine, "core", swap)


def step(
    fields,
    wet_bits,
    neighbours,
    kernel,
    conv_bias,
    ln_gain,
    ln_shift,
    in_weight,
    in_bias,
    out_weight,
    out_bias,
    cotangent,
):
    act2 = (C, CELLS)
    slot = lax.axis_index(TILE_AXES).astype(jnp.int32).reshape(1)
    core = lax.axis_index("core").astype(jnp.int32).reshape(1)
    cot = cotangent.reshape(act2)
    masked, wet = call(
        mask_kernel,
        [pltpu.VMEM(act2, bf16), pltpu.VMEM((8, CELLS), f32)],
        1,
        [wet_bits.transpose(2, 0, 1), fields.reshape(act2)],
        limit=4,
        n_far=2,
    )
    from_north = shifted(masked, 1)
    from_south = shifted(masked, -1)
    vectors = [v[None, :] for v in (conv_bias, ln_gain, ln_shift, out_bias)]
    high = lax.reduce_precision(in_bias, 8, 7)
    bias_rows = jnp.stack([high, in_bias - high]).astype(bf16)
    inwt = jnp.concatenate([in_weight, bias_rows, jnp.zeros((CX - C - 2, HID), bf16)], axis=0).T
    cot, inwt = lax.optimization_barrier((cot, inwt))
    table, masks, coef, chans, part, ograd, agrad, osum = call(
        pre_kernel,
        [
            pltpu.VMEM((C, COLS), f32),
            pltpu.VMEM((21, 8, COLS), f32),
            pltpu.VMEM((TAPS, C, COLS), f32),
            pltpu.VMEM((4, C, COLS), f32),
            pltpu.VMEM(act2, f32),
            pltpu.VMEM((CX, CELLS), bf16),
            pltpu.VMEM((HID, CELLS), f32),
            pltpu.VMEM((C, COLS), f32),
        ],
        2,
        [slot, neighbours, masked, wet, cot, kernel.T] + vectors + [out_weight],
        [((ROWS, C, COLS), f32), ((COLS, 2 * COLS), f32)],
        time=6.0,
        limit=8,
    )
    cgrad, act, keep, send, rows, vecs = call(
        main_kernel,
        [
            pltpu.VMEM(act2, bf16),
            pltpu.VMEM((HID, CELLS), bf16),
            pltpu.VMEM((HALF, COLS), bf16),
            pltpu.VMEM((HALF, COLS), bf16),
            pltpu.VMEM((4 * ROWS, C, COLS), f32),
            pltpu.VMEM((4, C, COLS), f32),
        ],
        1,
        [
            core,
            masked,
            from_north,
            from_south,
            masks,
            coef,
            chans,
            part,
            ograd,
            agrad,
            osum,
            in_weight,
            inwt,
        ],
        [
            (act2, f32),
            ((8, CELLS), f32),
            ((HID, CELLS), f32),
            ((CX, CELLS), bf16),
            ((HID, CELLS), bf16),
            ((8, COLS), f32),
            ((2, HALF, COLS), bf16),
        ],
        time=12.0,
        limit=20,
    )
    cg_north = shifted(cgrad, 1)
    cg_south = shifted(cgrad, -1)
    (small,) = call(
        taps_kernel,
        [pltpu.VMEM((C, COLS), f32)],
        0,
        [rows, masks, vecs],
        [((PAIRS, C, 2 * COLS), bf16), ((COLS, 2 * COLS), f32)],
        time=3.0,
        limit=12,
    )
    (field,) = call(
        field_kernel,
        [hbm(act2, bf16)],
        0,
        [masked, wet, table, act, out_weight.T],
        [(act2, f32)],
        time=1.5,
        limit=4,
    )
    (input_grad,) = call(
        back_kernel,
        [hbm(act2, bf16)],
        2,
        [slot, neighbours, cgrad, cg_north, cg_south, wet, cot, table],
        [((21, 8, COLS), f32), ((3 * ROWS, C, COLS), f32), (act2, f32), ((TAPS, C, COLS), f32)],
        time=6.0,
        limit=14,
    )
    mine, other = reduce_pack(keep, send, small)
    total_cells = lax.axis_size(TILE_AXES) * lax.axis_size("rep") * CELLS
    factor = float(total_cells) ** -0.5
    gin, gout, gkern, gbias, ggain, gshift, gobias, gibias = call(
        lambda *refs: unpack_kernel(factor, *refs),
        [hbm((C, HID), f32), hbm((C, HID), f32), hbm((TAPS, C), f32)] + [hbm((1, C), f32)] * 4 + [hbm((HID,), f32)],
        1,
        [core, mine, other],
        [((2, HALF, COLS), f32)],
        limit=8,
    )
    return (
        field.reshape(1, 1, C, CELLS),
        input_grad.reshape(1, 1, C, CELLS),
        gkern.T,
        gbias.reshape(C),
        ggain.reshape(C),
        gshift.reshape(C),
        gin,
        gibias,
        gout.T,
        gobias.reshape(C),
    )


def solution(mesh):
    rep = mesh.shape["rep"]
    fine = Mesh(mesh.devices.reshape(4, -1, 2, rep), ("y", "z", "core", "rep"))
    tile = P("rep", TILE_AXES, None, None)
    placed = (tile, P(TILE_AXES, None, None), P(TILE_AXES, None)) + (P(),) * 8 + (tile,)
    return jax.shard_map(
        step,
        mesh=fine,
        in_specs=placed,
        out_specs=(tile, tile) + (P(),) * 8,
        check_vma=False,
    )
```
